32 devices in a mesh: grp: 2 (over y), seq: 4 (over z), head: 2 (over x), sub: 2 (over core).
Axes of the slice: x: 2, y: 2, z: 4, core: 2. Of those that a mesh axis runs over, the one named last changes fastest.
Arguments:
- queries: float32 [1536, 2048], P(('grp', 'seq'), ('head', 'sub')), parts along dimension 0, may hold values from -6 to 6
- keys: float32 [1536, 2048], P(('grp', 'seq'), ('head', 'sub')), parts along dimension 0, may hold values from -6 to 6
- values: float32 [1536, 2048], P(('grp', 'seq'), ('head', 'sub')), parts along dimension 0, may hold values from -40 to 40
- opt_queries: float32 [16, 64, 2048], P(('grp', 'seq'), None, ('head', 'sub')), parts along dimension 0, may hold values from -6 to 6
- opt_keys: float32 [16, 64, 2048], P(('grp', 'seq'), None, ('head', 'sub')), parts along dimension 0, may hold values from -6 to 6
- opt_values: float32 [16, 64, 2048], P(('grp', 'seq'), None, ('head', 'sub')), parts along dimension 0, may hold values from -40 to 40
- opt_offsets: int32 [16], P(('grp', 'seq')), parts along dimension 0, may hold values from 0 to 192
- opt_lengths: int32 [16], P(('grp', 'seq')), parts along dimension 0, may hold values from 1 to 64, 320 in all
- norm_gain: float32 [2048], P(('head', 'sub')), may hold values from 0.5 to 2
- out_weight: bfloat16 [2048, 4096], P(('head', 'sub')), may hold values from -0.125 to 0.125
Outputs:
- ctx_out: bfloat16 [1536, 4096], P(('grp', 'seq'), ('head', 'sub')), parts along dimension 0
- opt_out: bfloat16 [16, 64, 4096], P(('grp', 'seq'), None, ('head', 'sub')), parts along dimension 0
The draws below stay inside these ranges and needn't reach their ends.
There are 2 independent parts, one for each index of `grp`. The reference program is written for one: setup_inputs(seed, part) draws one part's arguments, and reference() takes and returns one part's arrays. A program takes and returns all parts, laid end to end along the dimension named above; an argument that names none is the same for every part. Nothing has to cross between parts.
Inputs may be any that keep to these rules, and one draw needn't show every extreme that they name: `opt_lengths`: within each scoring group the 8 lengths sum to 320, and the longest option of each group has exactly 64 tokens in every draw.
All inputs are finite; a program needn't handle non-finite values.
Results may differ from the reference program's by a relative error of at most 0.017.
Values may be sent and summed in bfloat16 or wider, within the bound.
A program may use at most 64 MiB of HBM per device.

```python
import math
import jax
import jax.numpy as jnp
import numpy as np
from jax import lax

D = 4096
H = 16
DH = 128
TOK_DEV = 192
OPT_DEV = 2
OPT_LEN = 64
HD = 2048
CONTEXT = 768
OPTS = 8
N_SEQ = 4
N_HEAD = 2
N_SUB = 2


def scaled_values(key, shape):
    base_key, col_key, row_key = jax.random.split(key, 3)
    base = jnp.clip(jax.random.normal(base_key, shape, jnp.float32), -4.0, 4.0)
    col_scale = jnp.exp(jax.random.uniform(col_key, (shape[-1],), jnp.float32, 0.0, math.log(10.0)))
    row_scale = jnp.exp(jax.random.uniform(row_key, shape[:-1] + (1,), jnp.float32, 0.0, math.log(10.0)))
    return 0.1 * base * col_scale * row_scale


def draw_values(key, part):
    return scaled_values(jax.random.fold_in(key, 11), (CONTEXT, HD))


def draw_opt_values(key, part):
    return scaled_values(jax.random.fold_in(key, 23), (OPTS, OPT_LEN, HD))


def set_ends(array, own_key, low, largest):
    spot = [jax.random.randint(jax.random.fold_in(own_key, axis), (), 0, length) for axis, length in enumerate(array.shape)]
    main_axis = array.shape.index(max(array.shape))
    neighbour = spot[:main_axis] + [(spot[main_axis] + 1) % array.shape[main_axis]] + spot[main_axis + 1:]
    return array.at[tuple(spot)].set(low).at[tuple(neighbour)].set(largest)


def block_levels(key, extent, pieces, smallest, high):
    level, own = 1.0, jax.random.fold_in(key, 6)
    for axis_at, parts in pieces:
        heights = jnp.exp(jax.random.uniform(jax.random.fold_in(own, axis_at), (parts,), jnp.float32, smallest / len(pieces), high / len(pieces)))
        level = level * jnp.repeat(heights, extent[axis_at] // parts).reshape([-1 if axis == axis_at else 1 for axis in range(len(extent))])
    return level


def length_profile(amount, total, bound, skew):
    loads = [(1 << 20) // math.isqrt(grade ** skew) + 1 for grade in range(2, amount + 1)]
    rest, counts = total - bound - (amount - 1), [1] * (amount - 1)
    while rest > 0:
        movable = [i for i in range(amount - 1) if counts[i] < bound]
        whole, budget = sum([loads[i] for i in movable]), rest
        for i in movable:
            more = min(bound - counts[i], max(1, budget * loads[i] // whole), rest)
            counts[i] = counts[i] + more
            rest = rest - more
    return np.array([bound] + counts)


def ragged(key, amount, total, most, slope):
    if amount == 2:
        one = jax.random.randint(key, (), max(1, total - most), min(most, total - 1) + 1)
        return jnp.stack([one, total - one])
    tallies = jnp.asarray(length_profile(amount, total, most, slope), jnp.int32)
    twos = (amount - 1) // 2
    donor, taker = tallies[1:1 + 2 * twos:2], tallies[2:2 + 2 * twos:2]
    slack = jnp.minimum(donor - 1, most - taker)
    passed = jax.random.randint(jax.random.fold_in(key, 1), (twos,), 0, 1 << 20) % (slack + 1)
    tallies = tallies.at[1:1 + 2 * twos:2].set(donor - passed).at[2:2 + 2 * twos:2].set(taker + passed)
    return tallies[jax.random.permutation(jax.random.fold_in(key, 2), amount)]


def centred(key, shape, width, bound, pieces=(), kind=jnp.bfloat16):
    level = block_levels(key, shape, pieces, -0.22, 0.18) if pieces else 1.0
    values = jax.random.normal(key, shape, jnp.float32) * width * level
    return jnp.minimum(jnp.maximum(values, -bound), bound).astype(kind)


def setup_inputs(seed: int = 0, part: int = 0) -> dict:
    arg_keys = jax.random.split(jax.random.key(seed), 11)
    part_keys = jax.random.split(jax.random.fold_in(arg_keys[10], part), 11)
    queries = centred(part_keys[0], (CONTEXT, HD), 1.0, 6.0, ((0, 4), (1, 4)), jnp.float32)
    keys = centred(part_keys[1], (CONTEXT, HD), 1.0, 6.0, ((0, 4), (1, 4)), jnp.float32)
    values = draw_values(jax.random.fold_in(jax.random.fold_in(arg_keys[10], part), 71), part)
    opt_queries = centred(part_keys[3], (OPTS, OPT_LEN, HD), 1.0, 6.0, ((0, 4), (2, 4)), jnp.float32)
    opt_keys = centred(part_keys[4], (OPTS, OPT_LEN, HD), 1.0, 6.0, ((0, 4), (2, 4)), jnp.float32)
    opt_values = draw_opt_values(jax.random.fold_in(jax.random.fold_in(arg_keys[10], part), 71), part)
    opt_offsets = set_ends(jax.random.randint(part_keys[6], (OPTS,), 0, TOK_DEV + 1), jax.random.fold_in(part_keys[6], 1), 0, TOK_DEV).astype(jnp.int32)
    opt_lengths = ragged(part_keys[7], OPTS, OPTS * (OPT_LEN * 5 // 8), OPT_LEN, 1).astype(jnp.int32)
    norm_gain = jnp.clip(jnp.exp(math.log(2.0) - 1.3862944 * jax.random.uniform(arg_keys[8], (HD,), jnp.float32) ** block_levels(arg_keys[8], (HD,), ((0, 4),), -0.2, 0.2)), 0.5, 2.0)
    out_weight = centred(arg_keys[9], (HD, D), HD ** -0.5, 0.125, ((0, 4),))
    return {"queries": queries, "keys": keys, "values": values, "opt_queries": opt_queries, "opt_keys": opt_keys, "opt_values": opt_values, "opt_offsets": opt_offsets, "opt_lengths": opt_lengths, "norm_gain": norm_gain, "out_weight": out_weight}


norm_epsilon = 1e-05

def head_norm(attended, gain, mask):
    mean_square = lax.optimization_barrier(jnp.mean(attended * attended, axis=-1, keepdims=True))
    return (attended * lax.rsqrt(mean_square + norm_epsilon) * gain * mask).astype(jnp.bfloat16)

def project_groups(normed, weight_groups):
    groups = weight_groups.shape[0]
    flat = normed.reshape(normed.shape[0], groups, weight_groups.shape[1])
    partial_value = jnp.einsum('rgk,gkd->grd', flat.astype(jnp.float32), weight_groups.astype(jnp.float32), precision=lax.Precision.HIGHEST)
    partial_value = lax.optimization_barrier(partial_value.astype(jnp.bfloat16)).astype(jnp.float32)
    return lax.optimization_barrier(jnp.sum(partial_value, axis=0)).astype(jnp.bfloat16)

def reference(queries, keys, values, opt_queries, opt_keys, opt_values, opt_offsets, opt_lengths, norm_gain, out_weight):
    highest = lax.Precision.HIGHEST
    groups = N_HEAD * N_SUB
    query_blocks = queries.reshape(N_SEQ, TOK_DEV, H, DH)
    key_blocks = keys.reshape(N_SEQ, TOK_DEV, H, DH)
    value_blocks = values.reshape(N_SEQ, TOK_DEV, H, DH)
    states = jnp.einsum('cthd,cthe->chde', key_blocks, value_blocks, precision=highest)
    running = jnp.cumsum(states, axis=0)
    prefix = jnp.concatenate([jnp.zeros((1, H, DH, DH), jnp.float32), running[:-1]], axis=0)
    gain = norm_gain.reshape(H, DH)
    weight_groups = out_weight.reshape(groups, HD // groups, D)
    option_queries = opt_queries.reshape(N_SEQ, OPT_DEV, OPT_LEN, H, DH)
    option_keys = opt_keys.reshape(N_SEQ, OPT_DEV, OPT_LEN, H, DH)
    option_values = opt_values.reshape(N_SEQ, OPT_DEV, OPT_LEN, H, DH)
    offsets = opt_offsets.reshape(N_SEQ, OPT_DEV)
    lengths = opt_lengths.reshape(N_SEQ, OPT_DEV)
    positions = jnp.arange(TOK_DEV, dtype=jnp.int32)
    causal = (positions[:, None] >= positions[None, :]).astype(jnp.float32)
    slots = jnp.arange(OPT_LEN, dtype=jnp.int32)
    slot_causal = (slots[:, None] >= slots[None, :]).astype(jnp.float32)

    def one_block(inputs):
        block_q, block_k, block_v, block_prefix, opt_q, opt_k, opt_v, block_offsets, block_lengths = inputs
        inter = jnp.einsum('thd,hde->the', block_q, block_prefix, precision=highest)
        scores = jnp.einsum('thd,shd->hts', block_q, block_k, precision=highest) * causal[None]
        intra = jnp.einsum('hts,she->the', scores, block_v, precision=highest)
        context_normed = head_norm(inter + intra, gain, 1.0)
        context_rows = project_groups(context_normed.reshape(TOK_DEV, HD), weight_groups)
        before = (positions[None, :] < block_offsets[:, None]).astype(jnp.float32)
        local = jnp.einsum('ot,thd,the->ohde', before, block_k, block_v, precision=highest)
        opt_state = block_prefix[None] + local
        opt_inter = jnp.einsum('oihd,ohde->oihe', opt_q, opt_state, precision=highest)
        opt_scores = jnp.einsum('oihd,ojhd->ohij', opt_q, opt_k, precision=highest) * slot_causal[None, None]
        opt_intra = jnp.einsum('ohij,ojhe->oihe', opt_scores, opt_v, precision=highest)
        valid = (slots[None, :] < block_lengths[:, None]).astype(jnp.float32)
        opt_normed = head_norm(opt_inter + opt_intra, gain, valid[:, :, None, None])
        opt_rows = project_groups(opt_normed.reshape(OPT_DEV * OPT_LEN, HD), weight_groups)
        return (context_rows, opt_rows.reshape(OPT_DEV, OPT_LEN, D))
    context_out, option_out = lax.map(one_block, (query_blocks, key_blocks, value_blocks, prefix, option_queries, option_keys, option_values, offsets, lengths))
    return (context_out.reshape(CONTEXT, D), option_out.reshape(OPTS, OPT_LEN, D))
```

```python
import functools

import jax
import jax.numpy as jnp
from jax import lax
from jax.experimental import pallas as pl
from jax.experimental.pallas import tpu as pltpu
from jax.sharding import PartitionSpec as P

DH = 128
norm_epsilon = 1e-05
MESH = pl.DeviceIdType.MESH
bf16 = jnp.bfloat16
f32 = jnp.float32


def dot(a, b, ca, cb):
    return lax.dot_general(a, b, (((ca,), (cb,)), ((), ())), preferred_element_type=f32)


def kernel(
    sizes,
    q_hbm, k_hbm, v_hbm, oq_hbm, ok_hbm, ov_hbm, offs, lens, gain_ref, w_hbm,
    ctx_out, opt_out,
    q_buf, k_buf, v_buf, state, intra, pre_recv, pre_send, normed, sib_normed,
    w_own, w_sib, part_send, part_recv, own_part,
    in_sem, w_sem, ws_send, ws_recv, pre_ssem, pre_rsem, n_send, n_recv, x_send, x_recv,
):
    n_seq, n_head, n_sub, rows, opts, slots, chunks = sizes
    features = q_hbm.shape[1]
    heads = features // DH
    total = rows + opts * slots
    columns = w_own.shape[2]
    width = columns // chunks
    seq = lax.axis_index("seq")
    head = lax.axis_index("head")
    sub = lax.axis_index("sub")

    barrier = pltpu.get_barrier_semaphore()
    for e in range(1, n_sub):
        pl.semaphore_signal(
            barrier, inc=1, device_id={"sub": lax.rem(sub + e, n_sub)}, device_id_type=MESH
        )
    for d in range(1, n_head):
        pl.semaphore_signal(
            barrier, inc=1, device_id={"head": lax.rem(head + d, n_head)}, device_id_type=MESH
        )

    @pl.when(seq > 0)
    def _():
        pl.semaphore_signal(barrier, inc=1, device_id={"seq": seq - 1}, device_id_type=MESH)

    @pl.when(seq < n_seq - 1)
    def _():
        pl.semaphore_signal(barrier, inc=1, device_id={"seq": seq + 1}, device_id_type=MESH)

    loads = []
    for i, (src, dst, at, count) in enumerate((
        (k_hbm, k_buf, 0, rows),
        (v_hbm, v_buf, 0, rows),
        (q_hbm, q_buf, 0, rows),
        (ok_hbm, k_buf, rows, opts * slots),
        (oq_hbm, q_buf, rows, opts * slots),
        (ov_hbm, v_buf, rows, opts * slots),
    )):
        copy = pltpu.make_async_copy(src, dst.at[pl.ds(at, count)], in_sem.at[i])
        copy.start()
        loads.append(copy)

    def block_of(d, s):
        place = lax.rem(head + d, n_head) * n_sub + s
        return pl.ds(pl.multiple_of(place * columns, columns), columns)

    own_loads = []
    for d in range(n_head):
        copy = pltpu.make_async_copy(w_hbm.at[:, block_of(d, sub)], w_own.at[d], w_sem.at[d])
        own_loads.append(copy)

    def head_cols(h):
        return slice(h * DH, (h + 1) * DH)

    loads[0].wait()
    loads[1].wait()
    for h in range(heads):
        kh = k_buf[:rows, head_cols(h)].astype(bf16)
        vh = v_buf[:rows, head_cols(h)].astype(bf16)
        state[h] = dot(kh, vh, 0, 0)

    @pl.when(seq == 0)
    def _():
        for h in range(heads):
            pre_recv[h] = jnp.zeros((DH, DH), bf16)
            pre_send[h] = state[h].astype(bf16)

    greeted = (n_sub - 1) + (n_head - 1)
    around = jnp.where(seq > 0, 1, 0) + jnp.where(seq < n_seq - 1, 1, 0)
    pl.semaphore_wait(barrier, greeted + around)

    def pre_copy(h):
        return pltpu.make_async_remote_copy(
            src_ref=pre_send.at[h],
            dst_ref=pre_recv.at[h],
            send_sem=pre_ssem.at[h],
            recv_sem=pre_rsem.at[h],
            device_id={"seq": seq + 1},
            device_id_type=MESH,
        )

    @pl.when(jnp.logical_and(seq == 0, seq < n_seq - 1))
    def _():
        for h in range(heads):
            pre_copy(h).start()

    sib_copies = []
    for d in list(range(1, n_head)) + [0]:
        for e in range(1, n_sub):
            other = lax.rem(sub + e, n_sub)
            copy = pltpu.make_async_remote_copy(
                src_ref=w_hbm.at[:, block_of(d, other)],
                dst_ref=w_sib.at[e - 1, d],
                send_sem=ws_send.at[e - 1, d],
                recv_sem=ws_recv.at[e - 1, d],
                device_id={"sub": other},
                device_id_type=MESH,
            )
            copy.start()
            sib_copies.append(copy)
    for d in list(range(1, n_head)) + [0]:
        own_loads[d].start()

    for i in range(2, 6):
        loads[i].wait()

    ctx_mask = (
        lax.broadcasted_iota(jnp.int32, (rows, rows), 0)
        >= lax.broadcasted_iota(jnp.int32, (rows, rows), 1)
    )
    opt_masks = []
    for o in range(opts):
        col = lax.broadcasted_iota(jnp.int32, (slots, total), 1)
        row = lax.broadcasted_iota(jnp.int32, (slots, total), 0)
        first = rows + o * slots
        here = jnp.logical_and(col >= first, col <= row + first)
        opt_masks.append(jnp.logical_or(col < jnp.minimum(offs[o], rows), here))
    for h in range(heads):
        qh = q_buf[:, head_cols(h)].astype(bf16)
        kh = k_buf[:, head_cols(h)].astype(bf16)
        vh = v_buf[:, head_cols(h)].astype(bf16)
        scores = jnp.where(ctx_mask, dot(qh[:rows], kh[:rows], 1, 1), 0.0)
        intra[h, :rows] = dot(scores.astype(bf16), vh[:rows], 1, 0)
        opt_scores = dot(qh[rows:], kh, 1, 1)
        opt_scores = jnp.concatenate([
            jnp.where(opt_masks[o], opt_scores[o * slots:(o + 1) * slots], 0.0)
            for o in range(opts)
        ])
        intra[h, rows:] = dot(opt_scores.astype(bf16), vh, 1, 0)

    slot = lax.broadcasted_iota(jnp.int32, (slots, DH), 0)
    valid = [jnp.where(slot < lens[o], 1.0, 0.0) for o in range(opts)]

    n_copies = []
    for h in range(heads):
        @pl.when(seq > 0)
        def _():
            pre_copy(h).wait_recv()

            @pl.when(seq < n_seq - 1)
            def _():
                pre_send[h] = (state[h] + pre_recv[h].astype(f32)).astype(bf16)
                pre_copy(h).start()

        qh = q_buf[:, head_cols(h)].astype(bf16)
        att = intra[h] + dot(qh, pre_recv[h], 1, 0)
        square = jnp.mean(att * att, axis=-1, keepdims=True)
        out = att * lax.rsqrt(square + norm_epsilon) * gain_ref[:, head_cols(h)]
        normed[:rows, head_cols(h)] = out[:rows].astype(bf16)
        for o in range(opts):
            at = slice(rows + o * slots, rows + (o + 1) * slots)
            normed[at, head_cols(h)] = (out[at] * valid[o]).astype(bf16)
        for e in range(1, n_sub):
            copy = pltpu.make_async_remote_copy(
                src_ref=normed.at[:, pl.ds(h * DH, DH)],
                dst_ref=sib_normed.at[e - 1, :, pl.ds(h * DH, DH)],
                send_sem=n_send.at[e - 1, h],
                recv_sem=n_recv.at[e - 1, h],
                device_id={"sub": lax.rem(sub + e, n_sub)},
                device_id_type=MESH,
            )
            copy.start()
            n_copies.append(copy)

    for d in range(n_head):
        own_loads[d].wait()
    for copy in sib_copies:
        copy.wait_recv()
    for copy in n_copies:
        copy.wait_recv()

    def project(d, c):
        at = pl.ds(c * width, width)
        result = dot(normed[...], w_own[d, :, at], 1, 0)
        for e in range(n_sub - 1):
            result = result + dot(sib_normed[e], w_sib[e, d, :, at], 1, 0)
        return result

    x_copies = {}
    for c in range(chunks):
        for d in range(1, n_head):
            part_send[d - 1, c] = project(d, c).astype(bf16)
            copy = pltpu.make_async_remote_copy(
                src_ref=part_send.at[d - 1, c],
                dst_ref=part_recv.at[d - 1, c],
                send_sem=x_send.at[d - 1, c],
                recv_sem=x_recv.at[d - 1, c],
                device_id={"head": lax.rem(head + d, n_head)},
                device_id_type=MESH,
            )
            copy.start()
            x_copies[d, c] = copy
    for c in range(chunks):
        own_part[c] = project(0, c)
    for c in range(chunks):
        result = own_part[c]
        for d in range(1, n_head):
            x_copies[d, c].wait_recv()
            result = result + part_recv[d - 1, c].astype(f32)
        at = slice(c * width, (c + 1) * width)
        ctx_out[:, at] = result[:rows].astype(bf16)
        opt_out[:, at] = result[rows:].astype(bf16)

    for copy in list(x_copies.values()) + n_copies + sib_copies:
        copy.wait_send()

    @pl.when(seq < n_seq - 1)
    def _():
        for h in range(heads):
            pre_copy(h).wait_send()


def on_device(
    queries, keys, values, opt_queries, opt_keys, opt_values,
    opt_offsets, opt_lengths, norm_gain, out_weight,
):
    n_seq, n_head, n_sub = (lax.axis_size(a) for a in ("seq", "head", "sub"))
    rows, features = queries.shape
    opts, slots, _ = opt_queries.shape
    heads = features // DH
    total = rows + opts * slots
    columns = out_weight.shape[1] // (n_head * n_sub)
    width = 256 if columns % 256 == 0 else columns
    chunks = columns // width
    flat = lambda a: a.reshape(opts * slots, features)
    anyspace = pl.BlockSpec(memory_space=pl.ANY)
    vmem = pl.BlockSpec(memory_space=pltpu.VMEM)
    smem = pl.BlockSpec(memory_space=pltpu.SMEM)
    sem = pltpu.SemaphoreType.DMA
    ctx, opt = pl.pallas_call(
        functools.partial(kernel, (n_seq, n_head, n_sub, rows, opts, slots, chunks)),
        out_shape=(
            jax.ShapeDtypeStruct((rows, columns), bf16),
            jax.ShapeDtypeStruct((opts * slots, columns), bf16),
        ),
        in_specs=[anyspace] * 6 + [smem, smem, vmem, anyspace],
        out_specs=(vmem, vmem),
        scratch_shapes=[
            pltpu.VMEM((total, features), f32),
            pltpu.VMEM((total, features), f32),
            pltpu.VMEM((total, features), f32),
            pltpu.VMEM((heads, DH, DH), f32),
            pltpu.VMEM((heads, total, DH), f32),
            pltpu.VMEM((heads, DH, DH), bf16),
            pltpu.VMEM((heads, DH, DH), bf16),
            pltpu.VMEM((total, features), bf16),
            pltpu.VMEM((n_sub - 1, total, features), bf16),
            pltpu.VMEM((n_head, features, columns), bf16),
            pltpu.VMEM((n_sub - 1, n_head, features, columns), bf16),
            pltpu.VMEM((n_head - 1, chunks, total, width), bf16),
            pltpu.VMEM((n_head - 1, chunks, total, width), bf16),
            pltpu.VMEM((chunks, total, width), f32),
            sem((6,)),
            sem((n_head,)),
            sem((n_sub - 1, n_head)),
            sem((n_sub - 1, n_head)),
            sem((heads,)),
            sem((heads,)),
            sem((n_sub - 1, heads)),
            sem((n_sub - 1, heads)),
            sem((n_head - 1, chunks)),
            sem((n_head - 1, chunks)),
        ],
        compiler_params=pltpu.CompilerParams(collective_id=0, has_side_effects=True),
        name="scoring",
    )(
        queries, keys, values, flat(opt_queries), flat(opt_keys), flat(opt_values),
        opt_offsets, opt_lengths, norm_gain.reshape(1, features), out_weight,
    )
    return ctx, opt.reshape(opts, slots, columns)


def solution(mesh):
    placed = (
        P(("grp", "seq"), ("head", "sub")),
        P(("grp", "seq"), ("head", "sub")),
        P(("grp", "seq"), ("head", "sub")),
        P(("grp", "seq"), None, ("head", "sub")),
        P(("grp", "seq"), None, ("head", "sub")),
        P(("grp", "seq"), None, ("head", "sub")),
        P(("grp", "seq")),
        P(("grp", "seq")),
        P(("head", "sub")),
        P(("head", "sub"), None),
    )
    return jax.shard_map(
        on_device,
        mesh=mesh,
        in_specs=placed,
        out_specs=(P(("grp", "seq"), ("head", "sub")), P(("grp", "seq"), None, ("head", "sub"))),
        check_vma=False,
    )
```

```python
import functools

import jax
import jax.numpy as jnp
from jax import lax
from jax.experimental import pallas as pl
from jax.experimental.pallas import tpu as pltpu
from jax.sharding import PartitionSpec as P

DH = 128
norm_epsilon = 1e-05
MESH = pl.DeviceIdType.MESH
bf16 = jnp.bfloat16
f32 = jnp.float32


def dot(a, b, ca, cb):
    return lax.dot_general(a, b, (((ca,), (cb,)), ((), ())), preferred_element_type=f32)


def kernel(
    sizes,
    q_hbm, k_hbm, v_hbm, oq_hbm, ok_hbm, ov_hbm, offs, lens, gain_ref, w_hbm,
    ctx_out, opt_out,
    q_buf, k_buf, v_buf, state, intra, pre_recv, pre_send, normed, sib_normed,
    w_own, w_sib, part_send, part_recv, own_part,
    in_sem, w_sem, ws_send, ws_recv, pre_ssem, pre_rsem, n_send, n_recv, x_send, x_recv,
):
    n_seq, n_head, n_sub, rows, opts, slots, chunks = sizes
    features = q_hbm.shape[1]
    heads = features // DH
    total = rows + opts * slots
    columns = w_own.shape[2]
    width = columns // chunks
    seq = lax.axis_index("seq")
    head = lax.axis_index("head")
    sub = lax.axis_index("sub")

    barrier = pltpu.get_barrier_semaphore()
    for e in range(1, n_sub):
        pl.semaphore_signal(
            barrier, inc=1, device_id={"sub": lax.rem(sub + e, n_sub)}, device_id_type=MESH
        )
    for d in range(1, n_head):
        pl.semaphore_signal(
            barrier, inc=1, device_id={"head": lax.rem(head + d, n_head)}, device_id_type=MESH
        )

    @pl.when(seq > 0)
    def _():
        pl.semaphore_signal(barrier, inc=1, device_id={"seq": seq - 1}, device_id_type=MESH)

    @pl.when(seq < n_seq - 1)
    def _():
        pl.semaphore_signal(barrier, inc=1, device_id={"seq": seq + 1}, device_id_type=MESH)

    loads = []
    for i, (src, dst, at, count) in enumerate((
        (k_hbm, k_buf, 0, rows),
        (v_hbm, v_buf, 0, rows),
        (q_hbm, q_buf, 0, rows),
        (ok_hbm, k_buf, rows, opts * slots),
        (oq_hbm, q_buf, rows, opts * slots),
        (ov_hbm, v_buf, rows, opts * slots),
    )):
        copy = pltpu.make_async_copy(src, dst.at[pl.ds(at, count)], in_sem.at[i])
        copy.start()
        loads.append(copy)

    def block_of(d, s):
        place = lax.rem(head + d, n_head) * n_sub + s
        return pl.ds(pl.multiple_of(place * columns, columns), columns)

    own_loads = []
    for d in range(n_head):
        copy = pltpu.make_async_copy(w_hbm.at[:, block_of(d, sub)], w_own.at[d], w_sem.at[d])
        own_loads.append(copy)

    def head_cols(h):
        return slice(h * DH, (h + 1) * DH)

    loads[0].wait()
    loads[1].wait()
    for h in range(heads):
        kh = k_buf[:rows, head_cols(h)].astype(bf16)
        vh = v_buf[:rows, head_cols(h)].astype(bf16)
        state[h] = dot(kh, vh, 0, 0)

    @pl.when(seq == 0)
    def _():
        for h in range(heads):
            pre_recv[h] = jnp.zeros((DH, DH), bf16)
            pre_send[h] = state[h].astype(bf16)

    greeted = (n_sub - 1) + (n_head - 1)
    around = jnp.where(seq > 0, 1, 0) + jnp.where(seq < n_seq - 1, 1, 0)
    pl.semaphore_wait(barrier, greeted + around)

    def pre_copy(h):
        return pltpu.make_async_remote_copy(
            src_ref=pre_send.at[h],
            dst_ref=pre_recv.at[h],
            send_sem=pre_ssem.at[h],
            recv_sem=pre_rsem.at[h],
            device_id={"seq": seq + 1},
            device_id_type=MESH,
        )

    @pl.when(jnp.logical_and(seq == 0, seq < n_seq - 1))
    def _():
        for h in range(heads):
            pre_copy(h).start()

    sib_copies = []
    for d in list(range(1, n_head)) + [0]:
        for e in range(1, n_sub):
            other = lax.rem(sub + e, n_sub)
            copy = pltpu.make_async_remote_copy(
                src_ref=w_hbm.at[:, block_of(d, other)],
                dst_ref=w_sib.at[e - 1, d],
                send_sem=ws_send.at[e - 1, d],
                recv_sem=ws_recv.at[e - 1, d],
                device_id={"sub": other},
                device_id_type=MESH,
            )
            copy.start()
            sib_copies.append(copy)
    for d in list(range(1, n_head)) + [0]:
        own_loads[d].start()

    for i in range(2, 6):
        loads[i].wait()

    ctx_mask = (
        lax.broadcasted_iota(jnp.int32, (rows, rows), 0)
        >= lax.broadcasted_iota(jnp.int32, (rows, rows), 1)
    )
    opt_masks = []
    for o in range(opts):
        col = lax.broadcasted_iota(jnp.int32, (slots, total), 1)
        row = lax.broadcasted_iota(jnp.int32, (slots, total), 0)
        first = rows + o * slots
        here = jnp.logical_and(col >= first, col <= row + first)
        opt_masks.append(jnp.logical_or(col < jnp.minimum(offs[o], rows), here))
    def relay(h):
        pre_copy(h).wait_recv()

        @pl.when(seq < n_seq - 1)
        def _():
            pre_send[h] = (state[h] + pre_recv[h].astype(f32)).astype(bf16)
            pre_copy(h).start()

    for h in range(heads):
        qh = q_buf[:, head_cols(h)].astype(bf16)
        kh = k_buf[:, head_cols(h)].astype(bf16)
        vh = v_buf[:, head_cols(h)].astype(bf16)
        scores = jnp.where(ctx_mask, dot(qh[:rows], kh[:rows], 1, 1), 0.0)
        intra[h, :rows] = dot(scores.astype(bf16), vh[:rows], 1, 0)
        opt_scores = dot(qh[rows:], kh, 1, 1)
        opt_scores = jnp.concatenate([
            jnp.where(opt_masks[o], opt_scores[o * slots:(o + 1) * slots], 0.0)
            for o in range(opts)
        ])
        intra[h, rows:] = dot(opt_scores.astype(bf16), vh, 1, 0)

        @pl.when(seq == 1)
        def _():
            relay(h)

    slot = lax.broadcasted_iota(jnp.int32, (slots, DH), 0)
    valid = [jnp.where(slot < lens[o], 1.0, 0.0) for o in range(opts)]

    n_copies = []
    for h in range(heads):
        @pl.when(seq > 1)
        def _():
            relay(h)

        qh = q_buf[:, head_cols(h)].astype(bf16)
        att = intra[h] + dot(qh, pre_recv[h], 1, 0)
        square = jnp.mean(att * att, axis=-1, keepdims=True)
        out = att * lax.rsqrt(square + norm_epsilon) * gain_ref[:, head_cols(h)]
        normed[:rows, head_cols(h)] = out[:rows].astype(bf16)
        for o in range(opts):
            at = slice(rows + o * slots, rows + (o + 1) * slots)
            normed[at, head_cols(h)] = (out[at] * valid[o]).astype(bf16)
        for e in range(1, n_sub):
            copy = pltpu.make_async_remote_copy(
                src_ref=normed.at[:, pl.ds(h * DH, DH)],
                dst_ref=sib_normed.at[e - 1, :, pl.ds(h * DH, DH)],
                send_sem=n_send.at[e - 1, h],
                recv_sem=n_recv.at[e - 1, h],
                device_id={"sub": lax.rem(sub + e, n_sub)},
                device_id_type=MESH,
            )
            copy.start()
            n_copies.append(copy)

    for d in range(n_head):
        own_loads[d].wait()
    for copy in sib_copies:
        copy.wait_recv()
    for copy in n_copies:
        copy.wait_recv()

    def project(d, c):
        at = pl.ds(c * width, width)
        result = dot(normed[...], w_own[d, :, at], 1, 0)
        for e in range(n_sub - 1):
            result = result + dot(sib_normed[e], w_sib[e, d, :, at], 1, 0)
        return result

    x_copies = {}
    for c in range(chunks):
        for d in range(1, n_head):
            part_send[d - 1, c] = project(d, c).astype(bf16)
            copy = pltpu.make_async_remote_copy(
                src_ref=part_send.at[d - 1, c],
                dst_ref=part_recv.at[d - 1, c],
                send_sem=x_send.at[d - 1, c],
                recv_sem=x_recv.at[d - 1, c],
                device_id={"head": lax.rem(head + d, n_head)},
                device_id_type=MESH,
            )
            copy.start()
            x_copies[d, c] = copy
    for c in range(chunks):
        own_part[c] = project(0, c)
    for c in range(chunks):
        result = own_part[c]
        for d in range(1, n_head):
            x_copies[d, c].wait_recv()
            result = result + part_recv[d - 1, c].astype(f32)
        at = slice(c * width, (c + 1) * width)
        ctx_out[:, at] = result[:rows].astype(bf16)
        opt_out[:, at] = result[rows:].astype(bf16)

    for copy in list(x_copies.values()) + n_copies + sib_copies:
        copy.wait_send()

    @pl.when(seq < n_seq - 1)
    def _():
        for h in range(heads):
            pre_copy(h).wait_send()


def write_out(ctx, opt, ctx_hbm, opt_hbm, out_sem):
    copies = [
        pltpu.make_async_copy(ctx, ctx_hbm, out_sem.at[0]),
        pltpu.make_async_copy(opt, opt_hbm, out_sem.at[1]),
    ]
    for copy in copies:
        copy.start()
    for copy in copies:
        copy.wait()


def on_device(
    queries, keys, values, opt_queries, opt_keys, opt_values,
    opt_offsets, opt_lengths, norm_gain, out_weight,
):
    n_seq, n_head, n_sub = (lax.axis_size(a) for a in ("seq", "head", "sub"))
    rows, features = queries.shape
    opts, slots, _ = opt_queries.shape
    heads = features // DH
    total = rows + opts * slots
    columns = out_weight.shape[1] // (n_head * n_sub)
    width = 256 if columns % 256 == 0 else columns
    chunks = columns // width
    flat = lambda a: a.reshape(opts * slots, features)
    anyspace = pl.BlockSpec(memory_space=pl.ANY)
    vmem = pl.BlockSpec(memory_space=pltpu.VMEM)
    smem = pl.BlockSpec(memory_space=pltpu.SMEM)
    sem = pltpu.SemaphoreType.DMA
    ctx, opt = pl.pallas_call(
        functools.partial(kernel, (n_seq, n_head, n_sub, rows, opts, slots, chunks)),
        out_shape=(
            pltpu.VMEM((rows, columns), bf16),
            pltpu.VMEM((opts * slots, columns), bf16),
        ),
        in_specs=[anyspace] * 6 + [smem, smem, vmem, anyspace],
        out_specs=(vmem, vmem),
        scratch_shapes=[
            pltpu.VMEM((total, features), f32),
            pltpu.VMEM((total, features), f32),
            pltpu.VMEM((total, features), f32),
            pltpu.VMEM((heads, DH, DH), f32),
            pltpu.VMEM((heads, total, DH), f32),
            pltpu.VMEM((heads, DH, DH), bf16),
            pltpu.VMEM((heads, DH, DH), bf16),
            pltpu.VMEM((total, features), bf16),
            pltpu.VMEM((n_sub - 1, total, features), bf16),
            pltpu.VMEM((n_head, features, columns), bf16),
            pltpu.VMEM((n_sub - 1, n_head, features, columns), bf16),
            pltpu.VMEM((n_head - 1, chunks, total, width), bf16),
            pltpu.VMEM((n_head - 1, chunks, total, width), bf16),
            pltpu.VMEM((chunks, total, width), f32),
            sem((6,)),
            sem((n_head,)),
            sem((n_sub - 1, n_head)),
            sem((n_sub - 1, n_head)),
            sem((heads,)),
            sem((heads,)),
            sem((n_sub - 1, heads)),
            sem((n_sub - 1, heads)),
            sem((n_head - 1, chunks)),
            sem((n_head - 1, chunks)),
        ],
        compiler_params=pltpu.CompilerParams(collective_id=0, has_side_effects=True),
        name="scoring",
    )(
        queries, keys, values, flat(opt_queries), flat(opt_keys), flat(opt_values),
        opt_offsets, opt_lengths, norm_gain.reshape(1, features), out_weight,
    )
    ctx, opt = pl.pallas_call(
        write_out,
        out_shape=(
            jax.ShapeDtypeStruct((rows, columns), bf16),
            jax.ShapeDtypeStruct((opts * slots, columns), bf16),
        ),
        in_specs=[anyspace, anyspace],
        out_specs=(anyspace, anyspace),
        scratch_shapes=[sem((2,))],
        compiler_params=pltpu.CompilerParams(vmem_limit_bytes=1 << 20),
        name="write_out",
    )(ctx, opt)
    return ctx, opt.reshape(opts, slots, columns)


def solution(mesh):
    placed = (
        P(("grp", "seq"), ("head", "sub")),
        P(("grp", "seq"), ("head", "sub")),
        P(("grp", "seq"), ("head", "sub")),
        P(("grp", "seq"), None, ("head", "sub")),
        P(("grp", "seq"), None, ("head", "sub")),
        P(("grp", "seq"), None, ("head", "sub")),
        P(("grp", "seq")),
        P(("grp", "seq")),
        P(("head", "sub")),
        P(("head", "sub"), None),
    )
    return jax.shard_map(
        on_device,
        mesh=mesh,
        in_specs=placed,
        out_specs=(P(("grp", "seq"), ("head", "sub")), P(("grp", "seq"), None, ("head", "sub"))),
        check_vma=False,
    )
```

```python
import functools

import jax
import jax.numpy as jnp
from jax import lax
from jax.experimental import pallas as pl
from jax.experimental.pallas import tpu as pltpu
from jax.sharding import PartitionSpec as P

DH = 128
PIECES = 2
PIECE = DH // PIECES
norm_epsilon = 1e-05
MESH = pl.DeviceIdType.MESH
bf16 = jnp.bfloat16
f32 = jnp.float32


def dot(a, b, ca, cb):
    return lax.dot_general(a, b, (((ca,), (cb,)), ((), ())), preferred_element_type=f32)


def kernel(
    sizes,
    q_hbm, k_hbm, v_hbm, oq_hbm, ok_hbm, ov_hbm, offs_hbm, lens_hbm, gain_hbm, w_hbm,
    ctx_out, opt_out,
    q_buf, k_buf, v_buf, state, intra, pre_recv, pre_send, normed, sib_normed,
    w_own, w_sib, part_send, part_recv, own_part,
    offs, lens, gain_ref,
    in_sem, w_sem, ws_send, ws_recv, pre_ssem, pre_rsem, n_send, n_recv, x_send, x_recv,
):
    n_seq, n_head, n_sub, rows, opts, slots, chunks = sizes
    features = q_hbm.shape[1]
    heads = features // DH
    total = rows + opts * slots
    columns = w_own.shape[2]
    width = columns // chunks
    seq = lax.axis_index("seq")
    head = lax.axis_index("head")
    sub = lax.axis_index("sub")

    barrier = pltpu.get_barrier_semaphore()
    for e in range(1, n_sub):
        pl.semaphore_signal(
            barrier, inc=1, device_id={"sub": lax.rem(sub + e, n_sub)}, device_id_type=MESH
        )
    for d in range(1, n_head):
        pl.semaphore_signal(
            barrier, inc=1, device_id={"head": lax.rem(head + d, n_head)}, device_id_type=MESH
        )

    @pl.when(seq > 0)
    def _():
        pl.semaphore_signal(barrier, inc=1, device_id={"seq": seq - 1}, device_id_type=MESH)

    @pl.when(seq < n_seq - 1)
    def _():
        pl.semaphore_signal(barrier, inc=1, device_id={"seq": seq + 1}, device_id_type=MESH)

    loads = []
    for i, (src, dst, at, count) in enumerate((
        (k_hbm, k_buf, 0, rows),
        (v_hbm, v_buf, 0, rows),
        (q_hbm, q_buf, 0, rows),
        (ok_hbm, k_buf, rows, opts * slots),
        (oq_hbm, q_buf, rows, opts * slots),
        (ov_hbm, v_buf, rows, opts * slots),
    )):
        copy = pltpu.make_async_copy(src, dst.at[pl.ds(at, count)], in_sem.at[i])
        copy.start()
        loads.append(copy)
    for i, (src, dst) in enumerate(((offs_hbm, offs), (lens_hbm, lens), (gain_hbm, gain_ref))):
        copy = pltpu.make_async_copy(src, dst, in_sem.at[6 + i])
        copy.start()
        loads.append(copy)

    def block_of(d, s):
        place = lax.rem(head + d, n_head) * n_sub + s
        return pl.ds(pl.multiple_of(place * columns, columns), columns)

    own_loads = []
    for d in range(n_head):
        copy = pltpu.make_async_copy(w_hbm.at[:, block_of(d, sub)], w_own.at[d], w_sem.at[d])
        own_loads.append(copy)

    def head_cols(h):
        return slice(h * DH, (h + 1) * DH)

    loads[0].wait()
    loads[1].wait()
    for h in range(heads):
        kh = k_buf[:rows, head_cols(h)].astype(bf16)
        vh = v_buf[:rows, head_cols(h)].astype(bf16)
        state[h] = dot(kh, vh, 0, 0)

    @pl.when(seq == 0)
    def _():
        for h in range(heads):
            pre_recv[h] = jnp.zeros((DH, DH), bf16)
            pre_send[h] = state[h].astype(bf16)

    greeted = (n_sub - 1) + (n_head - 1)
    around = jnp.where(seq > 0, 1, 0) + jnp.where(seq < n_seq - 1, 1, 0)
    pl.semaphore_wait(barrier, greeted + around)

    def pre_copy(h, p):
        return pltpu.make_async_remote_copy(
            src_ref=pre_send.at[h, pl.ds(p * PIECE, PIECE)],
            dst_ref=pre_recv.at[h, pl.ds(p * PIECE, PIECE)],
            send_sem=pre_ssem.at[h, p],
            recv_sem=pre_rsem.at[h, p],
            device_id={"seq": seq + 1},
            device_id_type=MESH,
        )

    @pl.when(jnp.logical_and(seq == 0, seq < n_seq - 1))
    def _():
        for h in range(heads):
            for p in range(PIECES):
                pre_copy(h, p).start()

    sib_copies = []
    for d in list(range(1, n_head)) + [0]:
        for e in range(1, n_sub):
            other = lax.rem(sub + e, n_sub)
            copy = pltpu.make_async_remote_copy(
                src_ref=w_hbm.at[:, block_of(d, other)],
                dst_ref=w_sib.at[e - 1, d],
                send_sem=ws_send.at[e - 1, d],
                recv_sem=ws_recv.at[e - 1, d],
                device_id={"sub": other},
                device_id_type=MESH,
            )
            copy.start()
            sib_copies.append(copy)
    for d in list(range(1, n_head)) + [0]:
        own_loads[d].start()

    for i in range(2, 9):
        loads[i].wait()

    ctx_mask = (
        lax.broadcasted_iota(jnp.int32, (rows, rows), 0)
        >= lax.broadcasted_iota(jnp.int32, (rows, rows), 1)
    )
    opt_masks = []
    for o in range(opts):
        col = lax.broadcasted_iota(jnp.int32, (slots, total), 1)
        row = lax.broadcasted_iota(jnp.int32, (slots, total), 0)
        first = rows + o * slots
        here = jnp.logical_and(col >= first, col <= row + first)
        opt_masks.append(jnp.logical_or(col < jnp.minimum(offs[o], rows), here))
    def relay(h):
        for p in range(PIECES):
            pre_copy(h, p).wait_recv()

            @pl.when(seq < n_seq - 1)
            def _():
                at = slice(p * PIECE, (p + 1) * PIECE)
                pre_send[h, at] = (state[h, at] + pre_recv[h, at].astype(f32)).astype(bf16)
                pre_copy(h, p).start()

    for h in range(heads):
        qh = q_buf[:, head_cols(h)].astype(bf16)
        kh = k_buf[:, head_cols(h)].astype(bf16)
        vh = v_buf[:, head_cols(h)].astype(bf16)
        scores = jnp.where(ctx_mask, dot(qh[:rows], kh[:rows], 1, 1), 0.0)
        intra[h, :rows] = dot(scores.astype(bf16), vh[:rows], 1, 0)
        opt_scores = dot(qh[rows:], kh, 1, 1)
        opt_scores = jnp.concatenate([
            jnp.where(opt_masks[o], opt_scores[o * slots:(o + 1) * slots], 0.0)
            for o in range(opts)
        ])
        intra[h, rows:] = dot(opt_scores.astype(bf16), vh, 1, 0)

        @pl.when(seq == 1)
        def _():
            relay(h)

    slot = lax.broadcasted_iota(jnp.int32, (slots, DH), 0)
    valid = [jnp.where(slot < lens[o], 1.0, 0.0) for o in range(opts)]

    n_copies = []
    for h in range(heads):
        @pl.when(seq > 1)
        def _():
            relay(h)

        qh = q_buf[:, head_cols(h)].astype(bf16)
        att = intra[h] + dot(qh, pre_recv[h], 1, 0)
        square = jnp.mean(att * att, axis=-1, keepdims=True)
        out = att * lax.rsqrt(square + norm_epsilon) * gain_ref[:, head_cols(h)]
        normed[:rows, head_cols(h)] = out[:rows].astype(bf16)
        for o in range(opts):
            at = slice(rows + o * slots, rows + (o + 1) * slots)
            normed[at, head_cols(h)] = (out[at] * valid[o]).astype(bf16)
        for e in range(1, n_sub):
            copy = pltpu.make_async_remote_copy(
                src_ref=normed.at[:, pl.ds(h * DH, DH)],
                dst_ref=sib_normed.at[e - 1, :, pl.ds(h * DH, DH)],
                send_sem=n_send.at[e - 1, h],
                recv_sem=n_recv.at[e - 1, h],
                device_id={"sub": lax.rem(sub + e, n_sub)},
                device_id_type=MESH,
            )
            copy.start()
            n_copies.append(copy)

    for d in range(n_head):
        own_loads[d].wait()
    for copy in sib_copies:
        copy.wait_recv()
    for copy in n_copies:
        copy.wait_recv()

    def project(d, c):
        at = pl.ds(c * width, width)
        result = dot(normed[...], w_own[d, :, at], 1, 0)
        for e in range(n_sub - 1):
            result = result + dot(sib_normed[e], w_sib[e, d, :, at], 1, 0)
        return result

    x_copies = {}
    for c in range(chunks):
        for d in range(1, n_head):
            part_send[d - 1, c] = project(d, c).astype(bf16)
            copy = pltpu.make_async_remote_copy(
                src_ref=part_send.at[d - 1, c],
                dst_ref=part_recv.at[d - 1, c],
                send_sem=x_send.at[d - 1, c],
                recv_sem=x_recv.at[d - 1, c],
                device_id={"head": lax.rem(head + d, n_head)},
                device_id_type=MESH,
            )
            copy.start()
            x_copies[d, c] = copy
    for c in range(chunks):
        own_part[c] = project(0, c)
    for c in range(chunks):
        result = own_part[c]
        for d in range(1, n_head):
            x_copies[d, c].wait_recv()
            result = result + part_recv[d - 1, c].astype(f32)
        at = slice(c * width, (c + 1) * width)
        ctx_out[:, at] = result[:rows].astype(bf16)
        opt_out[:, at] = result[rows:].astype(bf16)

    for copy in list(x_copies.values()) + n_copies + sib_copies:
        copy.wait_send()

    @pl.when(seq < n_seq - 1)
    def _():
        for h in range(heads):
            for p in range(PIECES):
                pre_copy(h, p).wait_send()


def write_out(ctx, opt, ctx_hbm, opt_hbm, out_sem):
    copies = [
        pltpu.make_async_copy(ctx, ctx_hbm, out_sem.at[0]),
        pltpu.make_async_copy(opt, opt_hbm, out_sem.at[1]),
    ]
    for copy in copies:
        copy.start()
    for copy in copies:
        copy.wait()


def on_device(
    queries, keys, values, opt_queries, opt_keys, opt_values,
    opt_offsets, opt_lengths, norm_gain, out_weight,
):
    n_seq, n_head, n_sub = (lax.axis_size(a) for a in ("seq", "head", "sub"))
    rows, features = queries.shape
    opts, slots, _ = opt_queries.shape
    heads = features // DH
    total = rows + opts * slots
    columns = out_weight.shape[1] // (n_head * n_sub)
    width = 256 if columns % 256 == 0 else columns
    chunks = columns // width
    flat = lambda a: a.reshape(opts * slots, features)
    anyspace = pl.BlockSpec(memory_space=pl.ANY)
    vmem = pl.BlockSpec(memory_space=pltpu.VMEM)
    sem = pltpu.SemaphoreType.DMA
    ctx, opt = pl.pallas_call(
        functools.partial(kernel, (n_seq, n_head, n_sub, rows, opts, slots, chunks)),
        out_shape=(
            pltpu.VMEM((rows, columns), bf16),
            pltpu.VMEM((opts * slots, columns), bf16),
        ),
        in_specs=[anyspace] * 10,
        out_specs=(vmem, vmem),
        scratch_shapes=[
            pltpu.VMEM((total, features), f32),
            pltpu.VMEM((total, features), f32),
            pltpu.VMEM((total, features), f32),
            pltpu.VMEM((heads, DH, DH), f32),
            pltpu.VMEM((heads, total, DH), f32),
            pltpu.VMEM((heads, DH, DH), bf16),
            pltpu.VMEM((heads, DH, DH), bf16),
            pltpu.VMEM((total, features), bf16),
            pltpu.VMEM((n_sub - 1, total, features), bf16),
            pltpu.VMEM((n_head, features, columns), bf16),
            pltpu.VMEM((n_sub - 1, n_head, features, columns), bf16),
            pltpu.VMEM((n_head - 1, chunks, total, width), bf16),
            pltpu.VMEM((n_head - 1, chunks, total, width), bf16),
            pltpu.VMEM((chunks, total, width), f32),
            pltpu.SMEM((opts,), jnp.int32),
            pltpu.SMEM((opts,), jnp.int32),
            pltpu.VMEM((1, features), f32),
            sem((9,)),
            sem((n_head,)),
            sem((n_sub - 1, n_head)),
            sem((n_sub - 1, n_head)),
            sem((heads, PIECES)),
            sem((heads, PIECES)),
            sem((n_sub - 1, heads)),
            sem((n_sub - 1, heads)),
            sem((n_head - 1, chunks)),
            sem((n_head - 1, chunks)),
        ],
        compiler_params=pltpu.CompilerParams(collective_id=0, has_side_effects=True),
        name="scoring",
    )(
        queries, keys, values, flat(opt_queries), flat(opt_keys), flat(opt_values),
        opt_offsets, opt_lengths, norm_gain.reshape(1, features), out_weight,
    )
    ctx, opt = pl.pallas_call(
        write_out,
        out_shape=(
            jax.ShapeDtypeStruct((rows, columns), bf16),
            jax.ShapeDtypeStruct((opts * slots, columns), bf16),
        ),
        in_specs=[anyspace, anyspace],
        out_specs=(anyspace, anyspace),
        scratch_shapes=[sem((2,))],
        compiler_params=pltpu.CompilerParams(vmem_limit_bytes=1 << 20),
        name="write_out",
    )(ctx, opt)
    return ctx, opt.reshape(opts, slots, columns)


def solution(mesh):
    placed = (
        P(("grp", "seq"), ("head", "sub")),
        P(("grp", "seq"), ("head", "sub")),
        P(("grp", "seq"), ("head", "sub")),
        P(("grp", "seq"), None, ("head", "sub")),
        P(("grp", "seq"), None, ("head", "sub")),
        P(("grp", "seq"), None, ("head", "sub")),
        P(("grp", "seq")),
        P(("grp", "seq")),
        P(("head", "sub")),
        P(("head", "sub"), None),
    )
    return jax.shard_map(
        on_device,
        mesh=mesh,
        in_specs=placed,
        out_specs=(P(("grp", "seq"), ("head", "sub")), P(("grp", "seq"), None, ("head", "sub"))),
        check_vma=False,
    )
```

```python
import functools

import jax
import jax.numpy as jnp
from jax import lax
from jax.experimental import pallas as pl
from jax.experimental.pallas import tpu as pltpu
from jax.sharding import PartitionSpec as P

DH = 128
PIECES = 2
PIECE = DH // PIECES
norm_epsilon = 1e-05
MESH = pl.DeviceIdType.MESH
bf16 = jnp.bfloat16
f32 = jnp.float32


def dot(a, b, ca, cb):
    return lax.dot_general(a, b, (((ca,), (cb,)), ((), ())), preferred_element_type=f32)


def kernel(
    sizes,
    q_hbm, k_hbm, v_hbm, oq_hbm, ok_hbm, ov_hbm, offs_hbm, lens_hbm, gain_hbm, w_hbm,
    ctx_out, opt_out,
    q_buf, k_buf, v_buf, state, intra, pre_recv, pre_send, normed, sib_normed,
    w_own, w_sib, part_send, part_recv, own_part,
    offs, lens, gain_ref,
    in_sem, w_sem, ws_send, ws_recv, pre_ssem, pre_rsem, n_send, n_recv, x_send, x_recv,
):
    n_seq, n_head, n_sub, rows, opts, slots, chunks = sizes
    features = q_hbm.shape[1]
    heads = features // DH
    total = rows + opts * slots
    columns = w_own.shape[2]
    width = columns // chunks
    seq = lax.axis_index("seq")
    head = lax.axis_index("head")
    sub = lax.axis_index("sub")

    barrier = pltpu.get_barrier_semaphore()
    for e in range(1, n_sub):
        pl.semaphore_signal(
            barrier, inc=1, device_id={"sub": lax.rem(sub + e, n_sub)}, device_id_type=MESH
        )
    for d in range(1, n_head):
        pl.semaphore_signal(
            barrier, inc=1, device_id={"head": lax.rem(head + d, n_head)}, device_id_type=MESH
        )

    @pl.when(seq > 0)
    def _():
        pl.semaphore_signal(barrier, inc=1, device_id={"seq": seq - 1}, device_id_type=MESH)

    @pl.when(seq < n_seq - 1)
    def _():
        pl.semaphore_signal(barrier, inc=1, device_id={"seq": seq + 1}, device_id_type=MESH)

    loads = []
    for i, (src, dst, at, count) in enumerate((
        (k_hbm, k_buf, 0, rows),
        (v_hbm, v_buf, 0, rows),
        (q_hbm, q_buf, 0, rows),
        (ok_hbm, k_buf, rows, opts * slots),
        (oq_hbm, q_buf, rows, opts * slots),
        (ov_hbm, v_buf, rows, opts * slots),
    )):
        copy = pltpu.make_async_copy(src, dst.at[pl.ds(at, count)], in_sem.at[i])
        copy.start()
        loads.append(copy)
    for i, (src, dst) in enumerate(((offs_hbm, offs), (lens_hbm, lens), (gain_hbm, gain_ref))):
        copy = pltpu.make_async_copy(src, dst, in_sem.at[6 + i])
        copy.start()
        loads.append(copy)

    def block_of(d, s):
        place = lax.rem(head + d, n_head) * n_sub + s
        return pl.ds(pl.multiple_of(place * columns, columns), columns)

    own_loads = []
    for d in range(n_head):
        copy = pltpu.make_async_copy(w_hbm.at[:, block_of(d, sub)], w_own.at[d], w_sem.at[d])
        own_loads.append(copy)

    def head_cols(h):
        return slice(h * DH, (h + 1) * DH)

    loads[0].wait()
    loads[1].wait()
    for h in range(heads):
        kh = k_buf[:rows, head_cols(h)].astype(bf16)
        vh = v_buf[:rows, head_cols(h)].astype(bf16)
        state[h] = dot(kh, vh, 0, 0)

    @pl.when(seq == 0)
    def _():
        for h in range(heads):
            pre_recv[h] = jnp.zeros((DH, DH), bf16)
            pre_send[h] = state[h].astype(bf16)

    greeted = (n_sub - 1) + (n_head - 1)
    around = jnp.where(seq > 0, 1, 0) + jnp.where(seq < n_seq - 1, 1, 0)
    pl.semaphore_wait(barrier, greeted + around)

    def pre_copy(h, p):
        return pltpu.make_async_remote_copy(
            src_ref=pre_send.at[h, pl.ds(p * PIECE, PIECE)],
            dst_ref=pre_recv.at[h, pl.ds(p * PIECE, PIECE)],
            send_sem=pre_ssem.at[h, p],
            recv_sem=pre_rsem.at[h, p],
            device_id={"seq": seq + 1},
            device_id_type=MESH,
        )

    @pl.when(jnp.logical_and(seq == 0, seq < n_seq - 1))
    def _():
        for h in range(heads):
            for p in range(PIECES):
                pre_copy(h, p).start()

    sib_copies = []
    for d in list(range(1, n_head)) + [0]:
        for e in range(1, n_sub):
            other = lax.rem(sub + e, n_sub)
            copy = pltpu.make_async_remote_copy(
                src_ref=w_hbm.at[:, block_of(d, other)],
                dst_ref=w_sib.at[e - 1, d],
                send_sem=ws_send.at[e - 1, d],
                recv_sem=ws_recv.at[e - 1, d],
                device_id={"sub": other},
                device_id_type=MESH,
            )
            copy.start()
            sib_copies.append(copy)
    for d in list(range(1, n_head)) + [0]:
        own_loads[d].start()

    for i in range(2, 9):
        loads[i].wait()

    ctx_mask = (
        lax.broadcasted_iota(jnp.int32, (rows, rows), 0)
        >= lax.broadcasted_iota(jnp.int32, (rows, rows), 1)
    )
    opt_masks = []
    for o in range(opts):
        col = lax.broadcasted_iota(jnp.int32, (slots, total), 1)
        row = lax.broadcasted_iota(jnp.int32, (slots, total), 0)
        first = rows + o * slots
        here = jnp.logical_and(col >= first, col <= row + first)
        opt_masks.append(jnp.logical_or(col < jnp.minimum(offs[o], rows), here))
    def relay(h):
        for p in range(PIECES):
            pre_copy(h, p).wait_recv()

            @pl.when(seq < n_seq - 1)
            def _():
                at = slice(p * PIECE, (p + 1) * PIECE)
                pre_send[h, at] = (state[h, at] + pre_recv[h, at].astype(f32)).astype(bf16)
                pre_copy(h, p).start()

    for h in range(heads):
        qh = q_buf[:, head_cols(h)].astype(bf16)
        kh = k_buf[:, head_cols(h)].astype(bf16)
        vh = v_buf[:, head_cols(h)].astype(bf16)
        scores = jnp.where(ctx_mask, dot(qh[:rows], kh[:rows], 1, 1), 0.0)
        intra[h, :rows] = dot(scores.astype(bf16), vh[:rows], 1, 0)
        opt_scores = dot(qh[rows:], kh, 1, 1)
        opt_scores = jnp.concatenate([
            jnp.where(opt_masks[o], opt_scores[o * slots:(o + 1) * slots], 0.0)
            for o in range(opts)
        ])
        intra[h, rows:] = dot(opt_scores.astype(bf16), vh, 1, 0)

        @pl.when(seq == 1)
        def _():
            relay(h)

    slot = lax.broadcasted_iota(jnp.int32, (slots, DH), 0)
    valid = [jnp.where(slot < lens[o], 1.0, 0.0) for o in range(opts)]

    n_copies = []
    for h in range(heads):
        @pl.when(seq > 1)
        def _():
            relay(h)

        qh = q_buf[:, head_cols(h)].astype(bf16)
        att = intra[h] + dot(qh, pre_recv[h], 1, 0)
        square = jnp.mean(att * att, axis=-1, keepdims=True)
        out = att * lax.rsqrt(square + norm_epsilon) * gain_ref[:, head_cols(h)]
        normed[:rows, head_cols(h)] = out[:rows].astype(bf16)
        for o in range(opts):
            at = slice(rows + o * slots, rows + (o + 1) * slots)
            normed[at, head_cols(h)] = (out[at] * valid[o]).astype(bf16)
        for e in range(1, n_sub):
            copy = pltpu.make_async_remote_copy(
                src_ref=normed.at[:, pl.ds(h * DH, DH)],
                dst_ref=sib_normed.at[e - 1, :, pl.ds(h * DH, DH)],
                send_sem=n_send.at[e - 1, h],
                recv_sem=n_recv.at[e - 1, h],
                device_id={"sub": lax.rem(sub + e, n_sub)},
                device_id_type=MESH,
            )
            copy.start()
            n_copies.append(copy)

    for d in range(n_head):
        own_loads[d].wait()
    for copy in sib_copies:
        copy.wait_recv()
    half = max(heads // 2, 1)
    arrived = set()

    def wait_heads(first, last):
        for copy_h in range(first, last):
            for e in range(n_sub - 1):
                if (copy_h, e) not in arrived:
                    arrived.add((copy_h, e))
                    n_copies[copy_h * (n_sub - 1) + e].wait_recv()

    def project(d, c):
        at = pl.ds(c * width, width)
        result = dot(normed[...], w_own[d, :, at], 1, 0)
        for first, last in ((0, half), (half, heads)):
            wait_heads(first, last)
            part = slice(first * DH, last * DH)
            for e in range(n_sub - 1):
                result = result + dot(sib_normed[e, :, part], w_sib[e, d, part, at], 1, 0)
        return result

    x_copies = {}
    for c in range(chunks):
        for d in range(1, n_head):
            part_send[d - 1, c] = project(d, c).astype(bf16)
            copy = pltpu.make_async_remote_copy(
                src_ref=part_send.at[d - 1, c],
                dst_ref=part_recv.at[d - 1, c],
                send_sem=x_send.at[d - 1, c],
                recv_sem=x_recv.at[d - 1, c],
                device_id={"head": lax.rem(head + d, n_head)},
                device_id_type=MESH,
            )
            copy.start()
            x_copies[d, c] = copy
    for c in range(chunks):
        own_part[c] = project(0, c)
    for c in range(chunks):
        result = own_part[c]
        for d in range(1, n_head):
            x_copies[d, c].wait_recv()
            result = result + part_recv[d - 1, c].astype(f32)
        at = slice(c * width, (c + 1) * width)
        ctx_out[:, at] = result[:rows].astype(bf16)
        opt_out[:, at] = result[rows:].astype(bf16)

    for copy in list(x_copies.values()) + n_copies + sib_copies:
        copy.wait_send()

    @pl.when(seq < n_seq - 1)
    def _():
        for h in range(heads):
            for p in range(PIECES):
                pre_copy(h, p).wait_send()


def write_out(ctx, opt, ctx_hbm, opt_hbm, out_sem):
    copies = [
        pltpu.make_async_copy(ctx, ctx_hbm, out_sem.at[0]),
        pltpu.make_async_copy(opt, opt_hbm, out_sem.at[1]),
    ]
    for copy in copies:
        copy.start()
    for copy in copies:
        copy.wait()


def on_device(
    queries, keys, values, opt_queries, opt_keys, opt_values,
    opt_offsets, opt_lengths, norm_gain, out_weight,
):
    n_seq, n_head, n_sub = (lax.axis_size(a) for a in ("seq", "head", "sub"))
    rows, features = queries.shape
    opts, slots, _ = opt_queries.shape
    heads = features // DH
    total = rows + opts * slots
    columns = out_weight.shape[1] // (n_head * n_sub)
    width = 256 if columns % 256 == 0 else columns
    chunks = columns // width
    flat = lambda a: a.reshape(opts * slots, features)
    anyspace = pl.BlockSpec(memory_space=pl.ANY)
    vmem = pl.BlockSpec(memory_space=pltpu.VMEM)
    sem = pltpu.SemaphoreType.DMA
    ctx, opt = pl.pallas_call(
        functools.partial(kernel, (n_seq, n_head, n_sub, rows, opts, slots, chunks)),
        out_shape=(
            pltpu.VMEM((rows, columns), bf16),
            pltpu.VMEM((opts * slots, columns), bf16),
        ),
        in_specs=[anyspace] * 10,
        out_specs=(vmem, vmem),
        scratch_shapes=[
            pltpu.VMEM((total, features), f32),
            pltpu.VMEM((total, features), f32),
            pltpu.VMEM((total, features), f32),
            pltpu.VMEM((heads, DH, DH), f32),
            pltpu.VMEM((heads, total, DH), f32),
            pltpu.VMEM((heads, DH, DH), bf16),
            pltpu.VMEM((heads, DH, DH), bf16),
            pltpu.VMEM((total, features), bf16),
            pltpu.VMEM((n_sub - 1, total, features), bf16),
            pltpu.VMEM((n_head, features, columns), bf16),
            pltpu.VMEM((n_sub - 1, n_head, features, columns), bf16),
            pltpu.VMEM((n_head - 1, chunks, total, width), bf16),
            pltpu.VMEM((n_head - 1, chunks, total, width), bf16),
            pltpu.VMEM((chunks, total, width), f32),
            pltpu.SMEM((opts,), jnp.int32),
            pltpu.SMEM((opts,), jnp.int32),
            pltpu.VMEM((1, features), f32),
            sem((9,)),
            sem((n_head,)),
            sem((n_sub - 1, n_head)),
            sem((n_sub - 1, n_head)),
            sem((heads, PIECES)),
            sem((heads, PIECES)),
            sem((n_sub - 1, heads)),
            sem((n_sub - 1, heads)),
            sem((n_head - 1, chunks)),
            sem((n_head - 1, chunks)),
        ],
        compiler_params=pltpu.CompilerParams(collective_id=0, has_side_effects=True),
        name="scoring",
    )(
        queries, keys, values, flat(opt_queries), flat(opt_keys), flat(opt_values),
        opt_offsets, opt_lengths, norm_gain.reshape(1, features), out_weight,
    )
    ctx, opt = pl.pallas_call(
        write_out,
        out_shape=(
            jax.ShapeDtypeStruct((rows, columns), bf16),
            jax.ShapeDtypeStruct((opts * slots, columns), bf16),
        ),
        in_specs=[anyspace, anyspace],
        out_specs=(anyspace, anyspace),
        scratch_shapes=[sem((2,))],
        compiler_params=pltpu.CompilerParams(vmem_limit_bytes=1 << 20),
        name="write_out",
    )(ctx, opt)
    return ctx, opt.reshape(opts, slots, columns)


def solution(mesh):
    placed = (
        P(("grp", "seq"), ("head", "sub")),
        P(("grp", "seq"), ("head", "sub")),
        P(("grp", "seq"), ("head", "sub")),
        P(("grp", "seq"), None, ("head", "sub")),
        P(("grp", "seq"), None, ("head", "sub")),
        P(("grp", "seq"), None, ("head", "sub")),
        P(("grp", "seq")),
        P(("grp", "seq")),
        P(("head", "sub")),
        P(("head", "sub"), None),
    )
    return jax.shard_map(
        on_device,
        mesh=mesh,
        in_specs=placed,
        out_specs=(P(("grp", "seq"), ("head", "sub")), P(("grp", "seq"), None, ("head", "sub"))),
        check_vma=False,
    )
```

```python
import functools

import jax
import jax.numpy as jnp
from jax import lax
from jax.experimental import pallas as pl
from jax.experimental.pallas import tpu as pltpu
from jax.sharding import PartitionSpec as P

DH = 128
PIECES = 2
PIECE = DH // PIECES
norm_epsilon = 1e-05
MESH = pl.DeviceIdType.MESH
bf16 = jnp.bfloat16
f32 = jnp.float32


def dot(a, b, ca, cb):
    return lax.dot_general(a, b, (((ca,), (cb,)), ((), ())), preferred_element_type=f32)


def kernel(
    sizes,
    q_hbm, k_hbm, v_hbm, oq_hbm, ok_hbm, ov_hbm, offs_hbm, lens_hbm, gain_hbm, w_hbm,
    ctx_out, opt_out,
    q_buf, k_buf, v_buf, state, intra, pre_recv, pre_send, normed, sib_normed,
    w_own, w_sib, part_send, part_recv, own_part,
    offs, lens, gain_ref,
    in_sem, w_sem, ws_send, ws_recv, pre_ssem, pre_rsem, n_send, n_recv, x_send, x_recv,
):
    n_seq, n_head, n_sub, rows, opts, slots, chunks = sizes
    features = q_hbm.shape[1]
    heads = features // DH
    total = rows + opts * slots
    columns = w_own.shape[2]
    width = columns // chunks
    seq = lax.axis_index("seq")
    head = lax.axis_index("head")
    sub = lax.axis_index("sub")

    barrier = pltpu.get_barrier_semaphore()
    for e in range(1, n_sub):
        pl.semaphore_signal(
            barrier, inc=1, device_id={"sub": lax.rem(sub + e, n_sub)}, device_id_type=MESH
        )
    for d in range(1, n_head):
        pl.semaphore_signal(
            barrier, inc=1, device_id={"head": lax.rem(head + d, n_head)}, device_id_type=MESH
        )

    @pl.when(seq > 0)
    def _():
        pl.semaphore_signal(barrier, inc=1, device_id={"seq": seq - 1}, device_id_type=MESH)

    @pl.when(seq < n_seq - 1)
    def _():
        pl.semaphore_signal(barrier, inc=1, device_id={"seq": seq + 1}, device_id_type=MESH)

    loads = []
    for i, (src, dst, at, count) in enumerate((
        (k_hbm, k_buf, 0, rows),
        (v_hbm, v_buf, 0, rows),
        (q_hbm, q_buf, 0, rows),
        (ok_hbm, k_buf, rows, opts * slots),
        (oq_hbm, q_buf, rows, opts * slots),
        (ov_hbm, v_buf, rows, opts * slots),
    )):
        copy = pltpu.make_async_copy(src, dst.at[pl.ds(at, count)], in_sem.at[i])
        copy.start()
        loads.append(copy)
    for i, (src, dst) in enumerate(((offs_hbm, offs), (lens_hbm, lens), (gain_hbm, gain_ref))):
        copy = pltpu.make_async_copy(src, dst, in_sem.at[6 + i])
        copy.start()
        loads.append(copy)

    def block_of(d, s):
        place = lax.rem(head + d, n_head) * n_sub + s
        return pl.ds(pl.multiple_of(place * columns, columns), columns)

    own_loads = []
    for d in range(n_head):
        copy = pltpu.make_async_copy(w_hbm.at[:, block_of(d, sub)], w_own.at[d], w_sem.at[d])
        own_loads.append(copy)

    def head_cols(h):
        return slice(h * DH, (h + 1) * DH)

    loads[0].wait()
    loads[1].wait()
    for h in range(heads):
        kh = k_buf[:rows, head_cols(h)].astype(bf16)
        vh = v_buf[:rows, head_cols(h)].astype(bf16)
        state[h] = dot(kh, vh, 0, 0)

    @pl.when(seq == 0)
    def _():
        for h in range(heads):
            pre_recv[h] = jnp.zeros((DH, DH), bf16)
            pre_send[h] = state[h].astype(bf16)

    greeted = (n_sub - 1) + (n_head - 1)
    around = jnp.where(seq > 0, 1, 0) + jnp.where(seq < n_seq - 1, 1, 0)
    pl.semaphore_wait(barrier, greeted + around)

    def pre_copy(h, p):
        return pltpu.make_async_remote_copy(
            src_ref=pre_send.at[h, pl.ds(p * PIECE, PIECE)],
            dst_ref=pre_recv.at[h, pl.ds(p * PIECE, PIECE)],
            send_sem=pre_ssem.at[h, p],
            recv_sem=pre_rsem.at[h, p],
            device_id={"seq": seq + 1},
            device_id_type=MESH,
        )

    @pl.when(jnp.logical_and(seq == 0, seq < n_seq - 1))
    def _():
        for h in range(heads):
            for p in range(PIECES):
                pre_copy(h, p).start()

    sib_copies = []

    def fetch(d):
        for e in range(1, n_sub):
            other = lax.rem(sub + e, n_sub)
            copy = pltpu.make_async_remote_copy(
                src_ref=w_hbm.at[:, block_of(d, other)],
                dst_ref=w_sib.at[e - 1, d],
                send_sem=ws_send.at[e - 1, d],
                recv_sem=ws_recv.at[e - 1, d],
                device_id={"sub": other},
                device_id_type=MESH,
            )
            copy.start()
            sib_copies.append(copy)
        own_loads[d].start()

    def fetched(d):
        own_loads[d].wait()
        at = (n_head - 1 if d == 0 else d - 1) * (n_sub - 1)
        for copy in sib_copies[at:at + n_sub - 1]:
            copy.wait_recv()

    for d in range(1, n_head):
        fetch(d)

    for i in range(2, 9):
        loads[i].wait()

    ctx_mask = (
        lax.broadcasted_iota(jnp.int32, (rows, rows), 0)
        >= lax.broadcasted_iota(jnp.int32, (rows, rows), 1)
    )
    opt_masks = []
    for o in range(opts):
        col = lax.broadcasted_iota(jnp.int32, (slots, total), 1)
        row = lax.broadcasted_iota(jnp.int32, (slots, total), 0)
        first = rows + o * slots
        here = jnp.logical_and(col >= first, col <= row + first)
        opt_masks.append(jnp.logical_or(col < jnp.minimum(offs[o], rows), here))
    def relay(h):
        for p in range(PIECES):
            pre_copy(h, p).wait_recv()

            @pl.when(seq < n_seq - 1)
            def _():
                at = slice(p * PIECE, (p + 1) * PIECE)
                pre_send[h, at] = (state[h, at] + pre_recv[h, at].astype(f32)).astype(bf16)
                pre_copy(h, p).start()

    for h in range(heads):
        qh = q_buf[:, head_cols(h)].astype(bf16)
        kh = k_buf[:, head_cols(h)].astype(bf16)
        vh = v_buf[:, head_cols(h)].astype(bf16)
        scores = jnp.where(ctx_mask, dot(qh[:rows], kh[:rows], 1, 1), 0.0)
        intra[h, :rows] = dot(scores.astype(bf16), vh[:rows], 1, 0)
        opt_scores = dot(qh[rows:], kh, 1, 1)
        opt_scores = jnp.concatenate([
            jnp.where(opt_masks[o], opt_scores[o * slots:(o + 1) * slots], 0.0)
            for o in range(opts)
        ])
        intra[h, rows:] = dot(opt_scores.astype(bf16), vh, 1, 0)

        @pl.when(seq == 1)
        def _():
            relay(h)

    slot = lax.broadcasted_iota(jnp.int32, (slots, DH), 0)
    valid = [jnp.where(slot < lens[o], 1.0, 0.0) for o in range(opts)]

    n_copies = []
    for h in range(heads):
        @pl.when(seq > 1)
        def _():
            relay(h)

        qh = q_buf[:, head_cols(h)].astype(bf16)
        att = intra[h] + dot(qh, pre_recv[h], 1, 0)
        square = jnp.mean(att * att, axis=-1, keepdims=True)
        out = att * lax.rsqrt(square + norm_epsilon) * gain_ref[:, head_cols(h)]
        normed[:rows, head_cols(h)] = out[:rows].astype(bf16)
        for o in range(opts):
            at = slice(rows + o * slots, rows + (o + 1) * slots)
            normed[at, head_cols(h)] = (out[at] * valid[o]).astype(bf16)
        for e in range(1, n_sub):
            copy = pltpu.make_async_remote_copy(
                src_ref=normed.at[:, pl.ds(h * DH, DH)],
                dst_ref=sib_normed.at[e - 1, :, pl.ds(h * DH, DH)],
                send_sem=n_send.at[e - 1, h],
                recv_sem=n_recv.at[e - 1, h],
                device_id={"sub": lax.rem(sub + e, n_sub)},
                device_id_type=MESH,
            )
            copy.start()
            n_copies.append(copy)

    for d in range(1, n_head):
        fetched(d)
    half = max(heads // 2, 1)
    arrived = set()

    def wait_heads(first, last):
        for copy_h in range(first, last):
            for e in range(n_sub - 1):
                if (copy_h, e) not in arrived:
                    arrived.add((copy_h, e))
                    n_copies[copy_h * (n_sub - 1) + e].wait_recv()

    def project(d, c):
        at = pl.ds(c * width, width)
        result = dot(normed[...], w_own[d, :, at], 1, 0)
        for first, last in ((0, half), (half, heads)):
            wait_heads(first, last)
            part = slice(first * DH, last * DH)
            for e in range(n_sub - 1):
                result = result + dot(sib_normed[e, :, part], w_sib[e, d, part, at], 1, 0)
        return result

    x_copies = {}
    for c in range(chunks):
        for d in range(1, n_head):
            part_send[d - 1, c] = project(d, c).astype(bf16)
            copy = pltpu.make_async_remote_copy(
                src_ref=part_send.at[d - 1, c],
                dst_ref=part_recv.at[d - 1, c],
                send_sem=x_send.at[d - 1, c],
                recv_sem=x_recv.at[d - 1, c],
                device_id={"head": lax.rem(head + d, n_head)},
                device_id_type=MESH,
            )
            copy.start()
            x_copies[d, c] = copy
    fetch(0)
    fetched(0)
    for c in range(chunks):
        own_part[c] = project(0, c)
    for c in range(chunks):
        result = own_part[c]
        for d in range(1, n_head):
            x_copies[d, c].wait_recv()
            result = result + part_recv[d - 1, c].astype(f32)
        at = slice(c * width, (c + 1) * width)
        ctx_out[:, at] = result[:rows].astype(bf16)
        opt_out[:, at] = result[rows:].astype(bf16)

    for copy in list(x_copies.values()) + n_copies + sib_copies:
        copy.wait_send()

    @pl.when(seq < n_seq - 1)
    def _():
        for h in range(heads):
            for p in range(PIECES):
                pre_copy(h, p).wait_send()


def write_out(ctx, opt, ctx_hbm, opt_hbm, out_sem):
    copies = [
        pltpu.make_async_copy(ctx, ctx_hbm, out_sem.at[0]),
        pltpu.make_async_copy(opt, opt_hbm, out_sem.at[1]),
    ]
    for copy in copies:
        copy.start()
    for copy in copies:
        copy.wait()


def on_device(
    queries, keys, values, opt_queries, opt_keys, opt_values,
    opt_offsets, opt_lengths, norm_gain, out_weight,
):
    n_seq, n_head, n_sub = (lax.axis_size(a) for a in ("seq", "head", "sub"))
    rows, features = queries.shape
    opts, slots, _ = opt_queries.shape
    heads = features // DH
    total = rows + opts * slots
    columns = out_weight.shape[1] // (n_head * n_sub)
    width = 256 if columns % 256 == 0 else columns
    chunks = columns // width
    flat = lambda a: a.reshape(opts * slots, features)
    anyspace = pl.BlockSpec(memory_space=pl.ANY)
    vmem = pl.BlockSpec(memory_space=pltpu.VMEM)
    sem = pltpu.SemaphoreType.DMA
    ctx, opt = pl.pallas_call(
        functools.partial(kernel, (n_seq, n_head, n_sub, rows, opts, slots, chunks)),
        out_shape=(
            pltpu.VMEM((rows, columns), bf16),
            pltpu.VMEM((opts * slots, columns), bf16),
        ),
        in_specs=[anyspace] * 10,
        out_specs=(vmem, vmem),
        scratch_shapes=[
            pltpu.VMEM((total, features), f32),
            pltpu.VMEM((total, features), f32),
            pltpu.VMEM((total, features), f32),
            pltpu.VMEM((heads, DH, DH), f32),
            pltpu.VMEM((heads, total, DH), f32),
            pltpu.VMEM((heads, DH, DH), bf16),
            pltpu.VMEM((heads, DH, DH), bf16),
            pltpu.VMEM((total, features), bf16),
            pltpu.VMEM((n_sub - 1, total, features), bf16),
            pltpu.VMEM((n_head, features, columns), bf16),
            pltpu.VMEM((n_sub - 1, n_head, features, columns), bf16),
            pltpu.VMEM((n_head - 1, chunks, total, width), bf16),
            pltpu.VMEM((n_head - 1, chunks, total, width), bf16),
            pltpu.VMEM((chunks, total, width), f32),
            pltpu.SMEM((opts,), jnp.int32),
            pltpu.SMEM((opts,), jnp.int32),
            pltpu.VMEM((1, features), f32),
            sem((9,)),
            sem((n_head,)),
            sem((n_sub - 1, n_head)),
            sem((n_sub - 1, n_head)),
            sem((heads, PIECES)),
            sem((heads, PIECES)),
            sem((n_sub - 1, heads)),
            sem((n_sub - 1, heads)),
            sem((n_head - 1, chunks)),
            sem((n_head - 1, chunks)),
        ],
        compiler_params=pltpu.CompilerParams(collective_id=0, has_side_effects=True),
        name="scoring",
    )(
        queries, keys, values, flat(opt_queries), flat(opt_keys), flat(opt_values),
        opt_offsets, opt_lengths, norm_gain.reshape(1, features), out_weight,
    )
    ctx, opt = pl.pallas_call(
        write_out,
        out_shape=(
            jax.ShapeDtypeStruct((rows, columns), bf16),
            jax.ShapeDtypeStruct((opts * slots, columns), bf16),
        ),
        in_specs=[anyspace, anyspace],
        out_specs=(anyspace, anyspace),
        scratch_shapes=[sem((2,))],
        compiler_params=pltpu.CompilerParams(vmem_limit_bytes=1 << 20),
        name="write_out",
    )(ctx, opt)
    return ctx, opt.reshape(opts, slots, columns)


def solution(mesh):
    placed = (
        P(("grp", "seq"), ("head", "sub")),
        P(("grp", "seq"), ("head", "sub")),
        P(("grp", "seq"), ("head", "sub")),
        P(("grp", "seq"), None, ("head", "sub")),
        P(("grp", "seq"), None, ("head", "sub")),
        P(("grp", "seq"), None, ("head", "sub")),
        P(("grp", "seq")),
        P(("grp", "seq")),
        P(("head", "sub")),
        P(("head", "sub"), None),
    )
    return jax.shard_map(
        on_device,
        mesh=mesh,
        in_specs=placed,
        out_specs=(P(("grp", "seq"), ("head", "sub")), P(("grp", "seq"), None, ("head", "sub"))),
        check_vma=False,
    )
```

```python
import functools

import jax
import jax.numpy as jnp
from jax import lax
from jax.experimental import pallas as pl
from jax.experimental.pallas import tpu as pltpu
from jax.sharding import PartitionSpec as P

DH = 128
PIECES = 4
PIECE = DH // PIECES
norm_epsilon = 1e-05
MESH = pl.DeviceIdType.MESH
bf16 = jnp.bfloat16
f32 = jnp.float32


def dot(a, b, ca, cb):
    return lax.dot_general(a, b, (((ca,), (cb,)), ((), ())), preferred_element_type=f32)


def kernel(
    sizes,
    q_hbm, k_hbm, v_hbm, oq_hbm, ok_hbm, ov_hbm, offs_hbm, lens_hbm, gain_hbm, w_hbm,
    ctx_out, opt_out,
    q_buf, k_buf, v_buf, state, intra, pre_recv, pre_send, normed, sib_normed,
    w_own, w_sib, part_send, part_recv, own_part,
    offs, lens, gain_ref,
    in_sem, w_sem, ws_send, ws_recv, pre_ssem, pre_rsem, n_send, n_recv, x_send, x_recv,
):
    n_seq, n_head, n_sub, rows, opts, slots, chunks = sizes
    features = q_hbm.shape[1]
    heads = features // DH
    total = rows + opts * slots
    columns = w_own.shape[2]
    width = columns // chunks
    seq = lax.axis_index("seq")
    head = lax.axis_index("head")
    sub = lax.axis_index("sub")

    barrier = pltpu.get_barrier_semaphore()
    for e in range(1, n_sub):
        pl.semaphore_signal(
            barrier, inc=1, device_id={"sub": lax.rem(sub + e, n_sub)}, device_id_type=MESH
        )
    for d in range(1, n_head):
        pl.semaphore_signal(
            barrier, inc=1, device_id={"head": lax.rem(head + d, n_head)}, device_id_type=MESH
        )

    @pl.when(seq > 0)
    def _():
        pl.semaphore_signal(barrier, inc=1, device_id={"seq": seq - 1}, device_id_type=MESH)

    @pl.when(seq < n_seq - 1)
    def _():
        pl.semaphore_signal(barrier, inc=1, device_id={"seq": seq + 1}, device_id_type=MESH)

    loads = []
    for i, (src, dst, at, count) in enumerate((
        (k_hbm, k_buf, 0, rows),
        (v_hbm, v_buf, 0, rows),
        (q_hbm, q_buf, 0, rows),
        (ok_hbm, k_buf, rows, opts * slots),
        (oq_hbm, q_buf, rows, opts * slots),
        (ov_hbm, v_buf, rows, opts * slots),
    )):
        copy = pltpu.make_async_copy(src, dst.at[pl.ds(at, count)], in_sem.at[i])
        copy.start()
        loads.append(copy)
    for i, (src, dst) in enumerate(((offs_hbm, offs), (lens_hbm, lens), (gain_hbm, gain_ref))):
        copy = pltpu.make_async_copy(src, dst, in_sem.at[6 + i])
        copy.start()
        loads.append(copy)

    def block_of(d, s):
        place = lax.rem(head + d, n_head) * n_sub + s
        return pl.ds(pl.multiple_of(place * columns, columns), columns)

    own_loads = []
    for d in range(n_head):
        copy = pltpu.make_async_copy(w_hbm.at[:, block_of(d, sub)], w_own.at[d], w_sem.at[d])
        own_loads.append(copy)

    def head_cols(h):
        return slice(h * DH, (h + 1) * DH)

    loads[0].wait()
    loads[1].wait()
    for h in range(heads):
        kh = k_buf[:rows, head_cols(h)].astype(bf16)
        vh = v_buf[:rows, head_cols(h)].astype(bf16)
        state[h] = dot(kh, vh, 0, 0)

    @pl.when(seq == 0)
    def _():
        for h in range(heads):
            pre_recv[h] = jnp.zeros((DH, DH), bf16)
            pre_send[h] = state[h].astype(bf16)

    greeted = (n_sub - 1) + (n_head - 1)
    around = jnp.where(seq > 0, 1, 0) + jnp.where(seq < n_seq - 1, 1, 0)
    pl.semaphore_wait(barrier, greeted + around)

    def pre_copy(h, p):
        return pltpu.make_async_remote_copy(
            src_ref=pre_send.at[h, pl.ds(p * PIECE, PIECE)],
            dst_ref=pre_recv.at[h, pl.ds(p * PIECE, PIECE)],
            send_sem=pre_ssem.at[h, p],
            recv_sem=pre_rsem.at[h, p],
            device_id={"seq": seq + 1},
            device_id_type=MESH,
        )

    @pl.when(jnp.logical_and(seq == 0, seq < n_seq - 1))
    def _():
        for h in range(heads):
            for p in range(PIECES):
                pre_copy(h, p).start()

    sib_copies = []

    def fetch(d):
        for e in range(1, n_sub):
            other = lax.rem(sub + e, n_sub)
            copy = pltpu.make_async_remote_copy(
                src_ref=w_hbm.at[:, block_of(d, other)],
                dst_ref=w_sib.at[e - 1, d],
                send_sem=ws_send.at[e - 1, d],
                recv_sem=ws_recv.at[e - 1, d],
                device_id={"sub": other},
                device_id_type=MESH,
            )
            copy.start()
            sib_copies.append(copy)
        own_loads[d].start()

    def fetched(d):
        own_loads[d].wait()
        at = (n_head - 1 if d == 0 else d - 1) * (n_sub - 1)
        for copy in sib_copies[at:at + n_sub - 1]:
            copy.wait_recv()

    for d in range(1, n_head):
        fetch(d)

    for i in range(2, 9):
        loads[i].wait()

    ctx_mask = (
        lax.broadcasted_iota(jnp.int32, (rows, rows), 0)
        >= lax.broadcasted_iota(jnp.int32, (rows, rows), 1)
    )
    opt_masks = []
    for o in range(opts):
        col = lax.broadcasted_iota(jnp.int32, (slots, total), 1)
        row = lax.broadcasted_iota(jnp.int32, (slots, total), 0)
        first = rows + o * slots
        here = jnp.logical_and(col >= first, col <= row + first)
        opt_masks.append(jnp.logical_or(col < jnp.minimum(offs[o], rows), here))
    def relay(h):
        for p in range(PIECES):
            pre_copy(h, p).wait_recv()

            @pl.when(seq < n_seq - 1)
            def _():
                at = slice(p * PIECE, (p + 1) * PIECE)
                pre_send[h, at] = (state[h, at] + pre_recv[h, at].astype(f32)).astype(bf16)
                pre_copy(h, p).start()

    for h in range(heads):
        qh = q_buf[:, head_cols(h)].astype(bf16)
        kh = k_buf[:, head_cols(h)].astype(bf16)
        vh = v_buf[:, head_cols(h)].astype(bf16)
        scores = jnp.where(ctx_mask, dot(qh[:rows], kh[:rows], 1, 1), 0.0)
        intra[h, :rows] = dot(scores.astype(bf16), vh[:rows], 1, 0)
        opt_scores = dot(qh[rows:], kh, 1, 1)
        opt_scores = jnp.concatenate([
            jnp.where(opt_masks[o], opt_scores[o * slots:(o + 1) * slots], 0.0)
            for o in range(opts)
        ])
        intra[h, rows:] = dot(opt_scores.astype(bf16), vh, 1, 0)

        @pl.when(seq == 1)
        def _():
            relay(h)

    slot = lax.broadcasted_iota(jnp.int32, (slots, DH), 0)
    valid = [jnp.where(slot < lens[o], 1.0, 0.0) for o in range(opts)]

    n_copies = []
    for h in range(heads):
        @pl.when(seq > 1)
        def _():
            relay(h)

        qh = q_buf[:, head_cols(h)].astype(bf16)
        att = intra[h] + dot(qh, pre_recv[h], 1, 0)
        square = jnp.mean(att * att, axis=-1, keepdims=True)
        out = att * lax.rsqrt(square + norm_epsilon) * gain_ref[:, head_cols(h)]
        normed[:rows, head_cols(h)] = out[:rows].astype(bf16)
        for o in range(opts):
            at = slice(rows + o * slots, rows + (o + 1) * slots)
            normed[at, head_cols(h)] = (out[at] * valid[o]).astype(bf16)
        for e in range(1, n_sub):
            copy = pltpu.make_async_remote_copy(
                src_ref=normed.at[:, pl.ds(h * DH, DH)],
                dst_ref=sib_normed.at[e - 1, :, pl.ds(h * DH, DH)],
                send_sem=n_send.at[e - 1, h],
                recv_sem=n_recv.at[e - 1, h],
                device_id={"sub": lax.rem(sub + e, n_sub)},
                device_id_type=MESH,
            )
            copy.start()
            n_copies.append(copy)

    for d in range(1, n_head):
        fetched(d)
    half = max(heads // 2, 1)
    arrived = set()

    def wait_heads(first, last):
        for copy_h in range(first, last):
            for e in range(n_sub - 1):
                if (copy_h, e) not in arrived:
                    arrived.add((copy_h, e))
                    n_copies[copy_h * (n_sub - 1) + e].wait_recv()

    def project(d, c):
        at = pl.ds(c * width, width)
        result = dot(normed[...], w_own[d, :, at], 1, 0)
        for first, last in ((0, half), (half, heads)):
            wait_heads(first, last)
            part = slice(first * DH, last * DH)
            for e in range(n_sub - 1):
                result = result + dot(sib_normed[e, :, part], w_sib[e, d, part, at], 1, 0)
        return result

    x_copies = {}
    for c in range(chunks):
        for d in range(1, n_head):
            part_send[d - 1, c] = project(d, c).astype(bf16)
            copy = pltpu.make_async_remote_copy(
                src_ref=part_send.at[d - 1, c],
                dst_ref=part_recv.at[d - 1, c],
                send_sem=x_send.at[d - 1, c],
                recv_sem=x_recv.at[d - 1, c],
                device_id={"head": lax.rem(head + d, n_head)},
                device_id_type=MESH,
            )
            copy.start()
            x_copies[d, c] = copy
    fetch(0)
    fetched(0)
    for c in range(chunks):
        own_part[c] = project(0, c)
    for c in range(chunks):
        result = own_part[c]
        for d in range(1, n_head):
            x_copies[d, c].wait_recv()
            result = result + part_recv[d - 1, c].astype(f32)
        at = slice(c * width, (c + 1) * width)
        ctx_out[:, at] = result[:rows].astype(bf16)
        opt_out[:, at] = result[rows:].astype(bf16)

    for copy in list(x_copies.values()) + n_copies + sib_copies:
        copy.wait_send()

    @pl.when(seq < n_seq - 1)
    def _():
        for h in range(heads):
            for p in range(PIECES):
                pre_copy(h, p).wait_send()


def write_out(ctx, opt, ctx_hbm, opt_hbm, out_sem):
    copies = [
        pltpu.make_async_copy(ctx, ctx_hbm, out_sem.at[0]),
        pltpu.make_async_copy(opt, opt_hbm, out_sem.at[1]),
    ]
    for copy in copies:
        copy.start()
    for copy in copies:
        copy.wait()


def on_device(
    queries, keys, values, opt_queries, opt_keys, opt_values,
    opt_offsets, opt_lengths, norm_gain, out_weight,
):
    n_seq, n_head, n_sub = (lax.axis_size(a) for a in ("seq", "head", "sub"))
    rows, features = queries.shape
    opts, slots, _ = opt_queries.shape
    heads = features // DH
    total = rows + opts * slots
    columns = out_weight.shape[1] // (n_head * n_sub)
    width = 256 if columns % 256 == 0 else columns
    chunks = columns // width
    flat = lambda a: a.reshape(opts * slots, features)
    anyspace = pl.BlockSpec(memory_space=pl.ANY)
    vmem = pl.BlockSpec(memory_space=pltpu.VMEM)
    sem = pltpu.SemaphoreType.DMA
    ctx, opt = pl.pallas_call(
        functools.partial(kernel, (n_seq, n_head, n_sub, rows, opts, slots, chunks)),
        out_shape=(
            pltpu.VMEM((rows, columns), bf16),
            pltpu.VMEM((opts * slots, columns), bf16),
        ),
        in_specs=[anyspace] * 10,
        out_specs=(vmem, vmem),
        scratch_shapes=[
            pltpu.VMEM((total, features), f32),
            pltpu.VMEM((total, features), f32),
            pltpu.VMEM((total, features), f32),
            pltpu.VMEM((heads, DH, DH), f32),
            pltpu.VMEM((heads, total, DH), f32),
            pltpu.VMEM((heads, DH, DH), bf16),
            pltpu.VMEM((heads, DH, DH), bf16),
            pltpu.VMEM((total, features), bf16),
            pltpu.VMEM((n_sub - 1, total, features), bf16),
            pltpu.VMEM((n_head, features, columns), bf16),
            pltpu.VMEM((n_sub - 1, n_head, features, columns), bf16),
            pltpu.VMEM((n_head - 1, chunks, total, width), bf16),
            pltpu.VMEM((n_head - 1, chunks, total, width), bf16),
            pltpu.VMEM((chunks, total, width), f32),
            pltpu.SMEM((opts,), jnp.int32),
            pltpu.SMEM((opts,), jnp.int32),
            pltpu.VMEM((1, features), f32),
            sem((9,)),
            sem((n_head,)),
            sem((n_sub - 1, n_head)),
            sem((n_sub - 1, n_head)),
            sem((heads, PIECES)),
            sem((heads, PIECES)),
            sem((n_sub - 1, heads)),
            sem((n_sub - 1, heads)),
            sem((n_head - 1, chunks)),
            sem((n_head - 1, chunks)),
        ],
        compiler_params=pltpu.CompilerParams(collective_id=0, has_side_effects=True),
        name="scoring",
    )(
        queries, keys, values, flat(opt_queries), flat(opt_keys), flat(opt_values),
        opt_offsets, opt_lengths, norm_gain.reshape(1, features), out_weight,
    )
    ctx, opt = pl.pallas_call(
        write_out,
        out_shape=(
            jax.ShapeDtypeStruct((rows, columns), bf16),
            jax.ShapeDtypeStruct((opts * slots, columns), bf16),
        ),
        in_specs=[anyspace, anyspace],
        out_specs=(anyspace, anyspace),
        scratch_shapes=[sem((2,))],
        compiler_params=pltpu.CompilerParams(vmem_limit_bytes=1 << 20),
        name="write_out",
    )(ctx, opt)
    return ctx, opt.reshape(opts, slots, columns)


def solution(mesh):
    placed = (
        P(("grp", "seq"), ("head", "sub")),
        P(("grp", "seq"), ("head", "sub")),
        P(("grp", "seq"), ("head", "sub")),
        P(("grp", "seq"), None, ("head", "sub")),
        P(("grp", "seq"), None, ("head", "sub")),
        P(("grp", "seq"), None, ("head", "sub")),
        P(("grp", "seq")),
        P(("grp", "seq")),
        P(("head", "sub")),
        P(("head", "sub"), None),
    )
    return jax.shard_map(
        on_device,
        mesh=mesh,
        in_specs=placed,
        out_specs=(P(("grp", "seq"), ("head", "sub")), P(("grp", "seq"), None, ("head", "sub"))),
        check_vma=False,
    )
```

```python
import functools

import jax
import jax.numpy as jnp
from jax import lax
from jax.experimental import pallas as pl
from jax.experimental.pallas import tpu as pltpu
from jax.sharding import PartitionSpec as P

DH = 128
PIECES = 2
PIECE = DH // PIECES
norm_epsilon = 1e-05
MESH = pl.DeviceIdType.MESH
bf16 = jnp.bfloat16
f32 = jnp.float32


def dot(a, b, ca, cb):
    return lax.dot_general(a, b, (((ca,), (cb,)), ((), ())), preferred_element_type=f32)


def kernel(
    sizes,
    q_hbm, k_hbm, v_hbm, oq_hbm, ok_hbm, ov_hbm, offs_hbm, lens_hbm, gain_hbm, w_hbm,
    ctx_out, opt_out,
    q_buf, k_buf, v_buf, state, intra, pre_recv, pre_send, normed, sib_normed,
    w_own, w_sib, part_send, part_recv, own_part,
    offs, lens, gain_ref,
    in_sem, w_sem, ws_send, ws_recv, pre_ssem, pre_rsem, n_send, n_recv, x_send, x_recv,
):
    n_seq, n_head, n_sub, rows, opts, slots, chunks = sizes
    features = q_hbm.shape[1]
    heads = features // DH
    total = rows + opts * slots
    columns = w_own.shape[2]
    width = columns // chunks
    seq = lax.axis_index("seq")
    head = lax.axis_index("head")
    sub = lax.axis_index("sub")

    barrier = pltpu.get_barrier_semaphore()
    for e in range(1, n_sub):
        pl.semaphore_signal(
            barrier, inc=1, device_id={"sub": lax.rem(sub + e, n_sub)}, device_id_type=MESH
        )
    for d in range(1, n_head):
        pl.semaphore_signal(
            barrier, inc=1, device_id={"head": lax.rem(head + d, n_head)}, device_id_type=MESH
        )

    @pl.when(seq > 0)
    def _():
        pl.semaphore_signal(barrier, inc=1, device_id={"seq": seq - 1}, device_id_type=MESH)

    @pl.when(seq < n_seq - 1)
    def _():
        pl.semaphore_signal(barrier, inc=1, device_id={"seq": seq + 1}, device_id_type=MESH)

    loads = []
    for i, (src, dst, at, count) in enumerate((
        (k_hbm, k_buf, 0, rows),
        (v_hbm, v_buf, 0, rows),
        (q_hbm, q_buf, 0, rows),
        (ok_hbm, k_buf, rows, opts * slots),
        (oq_hbm, q_buf, rows, opts * slots),
        (ov_hbm, v_buf, rows, opts * slots),
    )):
        copy = pltpu.make_async_copy(src, dst.at[pl.ds(at, count)], in_sem.at[i])
        copy.start()
        loads.append(copy)
    for i, (src, dst) in enumerate(((offs_hbm, offs), (lens_hbm, lens), (gain_hbm, gain_ref))):
        copy = pltpu.make_async_copy(src, dst, in_sem.at[6 + i])
        copy.start()
        loads.append(copy)

    def block_of(d, s):
        place = lax.rem(head + d, n_head) * n_sub + s
        return pl.ds(pl.multiple_of(place * columns, columns), columns)

    own_loads = []
    for d in range(n_head):
        copy = pltpu.make_async_copy(w_hbm.at[:, block_of(d, sub)], w_own.at[d], w_sem.at[d])
        own_loads.append(copy)

    def head_cols(h):
        return slice(h * DH, (h + 1) * DH)

    loads[0].wait()
    loads[1].wait()
    for h in range(heads):
        kh = k_buf[:rows, head_cols(h)].astype(bf16)
        vh = v_buf[:rows, head_cols(h)].astype(bf16)
        state[h] = dot(kh, vh, 0, 0)

    @pl.when(seq == 0)
    def _():
        for h in range(heads):
            pre_recv[h] = jnp.zeros((DH, DH), bf16)
            pre_send[h] = state[h].astype(bf16)

    greeted = (n_sub - 1) + (n_head - 1)
    around = jnp.where(seq > 0, 1, 0) + jnp.where(seq < n_seq - 1, 1, 0)
    pl.semaphore_wait(barrier, greeted + around)

    def pre_copy(h, p):
        return pltpu.make_async_remote_copy(
            src_ref=pre_send.at[h, pl.ds(p * PIECE, PIECE)],
            dst_ref=pre_recv.at[h, pl.ds(p * PIECE, PIECE)],
            send_sem=pre_ssem.at[h, p],
            recv_sem=pre_rsem.at[h, p],
            device_id={"seq": seq + 1},
            device_id_type=MESH,
        )

    @pl.when(jnp.logical_and(seq == 0, seq < n_seq - 1))
    def _():
        for h in range(heads):
            for p in range(PIECES):
                pre_copy(h, p).start()

    sib_copies = []
    for d in list(range(1, n_head)) + [0]:
        for e in range(1, n_sub):
            other = lax.rem(sub + e, n_sub)
            copy = pltpu.make_async_remote_copy(
                src_ref=w_hbm.at[:, block_of(d, other)],
                dst_ref=w_sib.at[e - 1, d],
                send_sem=ws_send.at[e - 1, d],
                recv_sem=ws_recv.at[e - 1, d],
                device_id={"sub": other},
                device_id_type=MESH,
            )
            copy.start()
            sib_copies.append(copy)
    for d in list(range(1, n_head)) + [0]:
        own_loads[d].start()

    for i in range(2, 9):
        loads[i].wait()

    ctx_mask = (
        lax.broadcasted_iota(jnp.int32, (rows, rows), 0)
        >= lax.broadcasted_iota(jnp.int32, (rows, rows), 1)
    )
    opt_masks = []
    for o in range(opts):
        col = lax.broadcasted_iota(jnp.int32, (slots, total), 1)
        row = lax.broadcasted_iota(jnp.int32, (slots, total), 0)
        first = rows + o * slots
        here = jnp.logical_and(col >= first, col <= row + first)
        opt_masks.append(jnp.logical_or(col < jnp.minimum(offs[o], rows), here))
    def relay(h):
        for p in range(PIECES):
            pre_copy(h, p).wait_recv()

            @pl.when(seq < n_seq - 1)
            def _():
                at = slice(p * PIECE, (p + 1) * PIECE)
                pre_send[h, at] = (state[h, at] + pre_recv[h, at].astype(f32)).astype(bf16)
                pre_copy(h, p).start()

    for h in range(heads):
        qh = q_buf[:, head_cols(h)].astype(bf16)
        kh = k_buf[:, head_cols(h)].astype(bf16)
        vh = v_buf[:, head_cols(h)].astype(bf16)
        scores = jnp.where(ctx_mask, dot(qh[:rows], kh[:rows], 1, 1), 0.0)
        intra[h, :rows] = dot(scores.astype(bf16), vh[:rows], 1, 0)
        opt_scores = dot(qh[rows:], kh, 1, 1)
        opt_scores = jnp.concatenate([
            jnp.where(opt_masks[o], opt_scores[o * slots:(o + 1) * slots], 0.0)
            for o in range(opts)
        ])
        intra[h, rows:] = dot(opt_scores.astype(bf16), vh, 1, 0)

        @pl.when(seq == 1)
        def _():
            relay(h)

    slot = lax.broadcasted_iota(jnp.int32, (slots, DH), 0)
    valid = [jnp.where(slot < lens[o], 1.0, 0.0) for o in range(opts)]

    n_copies = []
    for h in range(heads):
        @pl.when(seq > 1)
        def _():
            relay(h)

        qh = q_buf[:, head_cols(h)].astype(bf16)
        att = intra[h] + dot(qh, pre_recv[h], 1, 0)
        square = jnp.mean(att * att, axis=-1, keepdims=True)
        out = att * lax.rsqrt(square + norm_epsilon) * gain_ref[:, head_cols(h)]
        normed[:rows, head_cols(h)] = out[:rows].astype(bf16)
        for o in range(opts):
            at = slice(rows + o * slots, rows + (o + 1) * slots)
            normed[at, head_cols(h)] = (out[at] * valid[o]).astype(bf16)
        for e in range(1, n_sub):
            copy = pltpu.make_async_remote_copy(
                src_ref=normed.at[:, pl.ds(h * DH, DH)],
                dst_ref=sib_normed.at[e - 1, :, pl.ds(h * DH, DH)],
                send_sem=n_send.at[e - 1, h],
                recv_sem=n_recv.at[e - 1, h],
                device_id={"sub": lax.rem(sub + e, n_sub)},
                device_id_type=MESH,
            )
            copy.start()
            n_copies.append(copy)

    for d in range(n_head):
        own_loads[d].wait()
    for copy in sib_copies:
        copy.wait_recv()
    half = max(heads // 2, 1)
    arrived = set()

    def wait_heads(first, last):
        for copy_h in range(first, last):
            for e in range(n_sub - 1):
                if (copy_h, e) not in arrived:
                    arrived.add((copy_h, e))
                    n_copies[copy_h * (n_sub - 1) + e].wait_recv()

    def project(d, c):
        at = pl.ds(c * width, width)
        result = dot(normed[...], w_own[d, :, at], 1, 0)
        for first, last in ((0, half), (half, heads)):
            wait_heads(first, last)
            part = slice(first * DH, last * DH)
            for e in range(n_sub - 1):
                result = result + dot(sib_normed[e, :, part], w_sib[e, d, part, at], 1, 0)
        return result

    x_copies = {}
    for c in range(chunks):
        for d in range(1, n_head):
            part_send[d - 1, c] = project(d, c).astype(bf16)
            copy = pltpu.make_async_remote_copy(
                src_ref=part_send.at[d - 1, c],
                dst_ref=part_recv.at[d - 1, c],
                send_sem=x_send.at[d - 1, c],
                recv_sem=x_recv.at[d - 1, c],
                device_id={"head": lax.rem(head + d, n_head)},
                device_id_type=MESH,
            )
            copy.start()
            x_copies[d, c] = copy
    for c in range(chunks):
        own_part[c] = project(0, c)
    for c in range(chunks):
        result = own_part[c]
        for d in range(1, n_head):
            x_copies[d, c].wait_recv()
            result = result + part_recv[d - 1, c].astype(f32)
        at = slice(c * width, (c + 1) * width)
        ctx_out[:, at] = result[:rows].astype(bf16)
        opt_out[:, at] = result[rows:].astype(bf16)

    for copy in list(x_copies.values()) + n_copies + sib_copies:
        copy.wait_send()

    @pl.when(seq < n_seq - 1)
    def _():
        for h in range(heads):
            for p in range(PIECES):
                pre_copy(h, p).wait_send()


def write_out(ctx, opt, ctx_hbm, opt_hbm, out_sem):
    copies = [
        pltpu.make_async_copy(ctx, ctx_hbm, out_sem.at[0]),
        pltpu.make_async_copy(opt, opt_hbm, out_sem.at[1]),
    ]
    for copy in copies:
        copy.start()
    for copy in copies:
        copy.wait()


def on_device(
    queries, keys, values, opt_queries, opt_keys, opt_values,
    opt_offsets, opt_lengths, norm_gain, out_weight,
):
    n_seq, n_head, n_sub = (lax.axis_size(a) for a in ("seq", "head", "sub"))
    rows, features = queries.shape
    opts, slots, _ = opt_queries.shape
    heads = features // DH
    total = rows + opts * slots
    columns = out_weight.shape[1] // (n_head * n_sub)
    width = 128 if columns % 128 == 0 else columns
    chunks = columns // width
    flat = lambda a: a.reshape(opts * slots, features)
    anyspace = pl.BlockSpec(memory_space=pl.ANY)
    vmem = pl.BlockSpec(memory_space=pltpu.VMEM)
    sem = pltpu.SemaphoreType.DMA
    ctx, opt = pl.pallas_call(
        functools.partial(kernel, (n_seq, n_head, n_sub, rows, opts, slots, chunks)),
        out_shape=(
            pltpu.VMEM((rows, columns), bf16),
            pltpu.VMEM((opts * slots, columns), bf16),
        ),
        in_specs=[anyspace] * 10,
        out_specs=(vmem, vmem),
        scratch_shapes=[
            pltpu.VMEM((total, features), f32),
            pltpu.VMEM((total, features), f32),
            pltpu.VMEM((total, features), f32),
            pltpu.VMEM((heads, DH, DH), f32),
            pltpu.VMEM((heads, total, DH), f32),
            pltpu.VMEM((heads, DH, DH), bf16),
            pltpu.VMEM((heads, DH, DH), bf16),
            pltpu.VMEM((total, features), bf16),
            pltpu.VMEM((n_sub - 1, total, features), bf16),
            pltpu.VMEM((n_head, features, columns), bf16),
            pltpu.VMEM((n_sub - 1, n_head, features, columns), bf16),
            pltpu.VMEM((n_head - 1, chunks, total, width), bf16),
            pltpu.VMEM((n_head - 1, chunks, total, width), bf16),
            pltpu.VMEM((chunks, total, width), f32),
            pltpu.SMEM((opts,), jnp.int32),
            pltpu.SMEM((opts,), jnp.int32),
            pltpu.VMEM((1, features), f32),
            sem((9,)),
            sem((n_head,)),
            sem((n_sub - 1, n_head)),
            sem((n_sub - 1, n_head)),
            sem((heads, PIECES)),
            sem((heads, PIECES)),
            sem((n_sub - 1, heads)),
            sem((n_sub - 1, heads)),
            sem((n_head - 1, chunks)),
            sem((n_head - 1, chunks)),
        ],
        compiler_params=pltpu.CompilerParams(collective_id=0, has_side_effects=True),
        name="scoring",
    )(
        queries, keys, values, flat(opt_queries), flat(opt_keys), flat(opt_values),
        opt_offsets, opt_lengths, norm_gain.reshape(1, features), out_weight,
    )
    ctx, opt = pl.pallas_call(
        write_out,
        out_shape=(
            jax.ShapeDtypeStruct((rows, columns), bf16),
            jax.ShapeDtypeStruct((opts * slots, columns), bf16),
        ),
        in_specs=[anyspace, anyspace],
        out_specs=(anyspace, anyspace),
        scratch_shapes=[sem((2,))],
        compiler_params=pltpu.CompilerParams(vmem_limit_bytes=1 << 20),
        name="write_out",
    )(ctx, opt)
    return ctx, opt.reshape(opts, slots, columns)


def solution(mesh):
    placed = (
        P(("grp", "seq"), ("head", "sub")),
        P(("grp", "seq"), ("head", "sub")),
        P(("grp", "seq"), ("head", "sub")),
        P(("grp", "seq"), None, ("head", "sub")),
        P(("grp", "seq"), None, ("head", "sub")),
        P(("grp", "seq"), None, ("head", "sub")),
        P(("grp", "seq")),
        P(("grp", "seq")),
        P(("head", "sub")),
        P(("head", "sub"), None),
    )
    return jax.shard_map(
        on_device,
        mesh=mesh,
        in_specs=placed,
        out_specs=(P(("grp", "seq"), ("head", "sub")), P(("grp", "seq"), None, ("head", "sub"))),
        check_vma=False,
    )
```
